256 devices in a mesh: gx: 8 (over y, core), gy: 4 (over z_hi), gz: 8 (over z_lo, x).
Axes of the slice: x: 4, y: 4, z: 8 (z_hi: 4, z_lo: 2; z = z_hi * 2 + z_lo), core: 2. Of those that a mesh axis runs over, the one named last changes fastest.
Arguments:
- features: float32 [8, 4, 16, 64, 128], P('gx', 'gy', 'gz'), may hold values from -6 to 6
- positions: float32 [8, 4, 16, 3, 64], P('gx', 'gy', 'gz'), may hold values from 0 to 8
- counts: int32 [8, 4, 16], P('gx', 'gy', 'gz'), may hold values from 40 to 64, as said below
- rbf_weight: bfloat16 [2, 64, 128], replicated, may hold values from -2 to 2
- rbf_bias: float32 [2, 128], replicated, may hold values from -3 to 3
- filter_weight: bfloat16 [2, 128, 128], replicated, may hold values from -0.5 to 0.5
- filter_bias: float32 [2, 128], replicated, may hold values from -3 to 3
- input_weight: float32 [2, 128, 128], replicated, may hold values from -0.5 to 0.5
- output_weight: float32 [2, 128, 128], replicated, may hold values from -0.5 to 0.5
- output_bias: float32 [2, 128], replicated, may hold values from -3 to 3
- final_weight: float32 [2, 128, 128], replicated, may hold values from -0.5 to 0.5
- final_bias: float32 [2, 128], replicated, may hold values from -3 to 3
Outputs:
- refined: float32 [8, 4, 16, 64, 128], P('gx', 'gy', 'gz')
The draws below stay inside these ranges and needn't reach their ends.
Inputs may be any that keep to these rules, and one draw needn't show every extreme that they name: `counts`: slots below a cell's count hold atoms and the others are padding; some cell holds 64 atoms in every draw.
All inputs are finite; a program needn't handle non-finite values.
Results may differ from the reference program's by a relative error of at most 0.00045.
Values sent between devices are 32-bit elements; how exact they have to be, the bound alone decides.
A program may use at most 64 MiB of HBM per device.

```python
import math
from functools import partial
import jax
import jax.numpy as jnp
from jax import lax

F = 128
RBF = 64
ATOMS = 64
BLOCKS = 2
NX = 8
NY = 4
NZ = 16


def draw_counts(key, part):
    lowest = ATOMS * 5 // 8
    spread = ATOMS - lowest
    first, second = jax.random.split(key)
    drawn = jax.random.randint(first, (NX * NY * NZ,), 0, spread + 1)
    amounts = lowest + drawn * drawn // spread
    chosen = jax.random.randint(second, (), 0, NX * NY * NZ)
    amounts = jnp.where(jnp.arange(NX * NY * NZ) == chosen, ATOMS, amounts)
    return amounts.reshape(NX, NY, NZ).astype(jnp.int32)


def shard_levels(rng, dims, cuts, least, largest):
    factor_of = 1.0
    for axis_at, shards_of in cuts:
        steps = jax.random.uniform(jax.random.fold_in(jax.random.fold_in(rng, 6), axis_at), (shards_of,), jnp.float32, least / len(cuts), largest / len(cuts))
        factor_of = factor_of * jnp.repeat(jnp.exp(steps), dims[axis_at] // shards_of).reshape((-1,) + (1,) * (len(dims) - 1 - axis_at))
    return factor_of


def bell_draw(own_key, shape, scale, most, cuts=(), kind=jnp.bfloat16):
    factor_of = shard_levels(own_key, shape, cuts, -0.22, 0.18) if cuts else 1.0
    values = jax.random.normal(own_key, shape, jnp.float32) * scale * factor_of
    return jnp.minimum(jnp.maximum(values, -most), most).astype(kind)


def setup_inputs(seed: int = 0) -> dict:
    splits = jax.random.split(jax.random.key(seed), 13)
    features = bell_draw(splits[0], (NX, NY, NZ, ATOMS, F), 1.0, 6.0, ((0, 8), (1, 4), (2, 8)), jnp.float32)
    positions = jnp.clip(8.0 * jax.random.uniform(splits[1], (NX, NY, NZ, 3, ATOMS), jnp.float32) ** shard_levels(splits[1], (NX, NY, NZ, 3, ATOMS), ((0, 8), (1, 4), (2, 8)), -0.2, 0.2), 0.0, 8.0)
    counts = draw_counts(jax.random.fold_in(splits[12], 71), 0)
    rbf_weight = bell_draw(splits[3], (BLOCKS, RBF, F), (RBF // 8) ** -0.5, 2.0)
    rbf_bias = bell_draw(splits[4], (BLOCKS, F), 0.5, 3.0, (), jnp.float32)
    filter_weight = bell_draw(splits[5], (BLOCKS, F, F), F ** -0.5, 0.5)
    filter_bias = bell_draw(splits[6], (BLOCKS, F), 0.5, 3.0, (), jnp.float32)
    input_weight = bell_draw(splits[7], (BLOCKS, F, F), F ** -0.5, 0.5, (), jnp.float32)
    output_weight = bell_draw(splits[8], (BLOCKS, F, F), F ** -0.5, 0.5, (), jnp.float32)
    output_bias = bell_draw(splits[9], (BLOCKS, F), 0.5, 3.0, (), jnp.float32)
    final_weight = bell_draw(splits[10], (BLOCKS, F, F), F ** -0.5, 0.5, (), jnp.float32)
    final_bias = bell_draw(splits[11], (BLOCKS, F), 0.5, 3.0, (), jnp.float32)
    return dict(features=features, positions=positions, counts=counts, rbf_weight=rbf_weight, rbf_bias=rbf_bias, filter_weight=filter_weight, filter_bias=filter_bias, input_weight=input_weight, output_weight=output_weight, output_bias=output_bias, final_weight=final_weight, final_bias=final_bias)


cell_edge = 8.0
cutoff = 5.0
gamma = 10.0
scale_sum = 0.125

def shifted_softplus(value):
    return jax.nn.softplus(value) - math.log(2.0)

def half_offsets():
    listing = []
    for step_x in (-1, 0, 1):
        for step_y in (-1, 0, 1):
            for step_z in (-1, 0, 1):
                offset = (step_x, step_y, step_z)
                if offset >= (0, 0, 0):
                    listing.append(offset)
    return listing

def pair_tile(pos_own, live_own, value_own, pos_near, live_near, value_near, offset_vec, self_flag, weights):
    rbf_w, rbf_b, filt_w, filt_b = weights
    delta = pos_near[:, None, :] + (cell_edge * offset_vec)[:, None, None] - pos_own[:, :, None]
    distance = jnp.sqrt(lax.optimization_barrier(jnp.sum(delta * delta, axis=0)))
    centres = jnp.arange(RBF, dtype=jnp.float32) * (cutoff / (RBF - 1))
    apart = distance[:, :, None] - centres
    radial = jnp.exp(-gamma * apart * apart).astype(jnp.bfloat16).reshape(ATOMS * ATOMS, RBF)
    hidden = shifted_softplus(jnp.dot(radial, rbf_w, preferred_element_type=jnp.float32) + rbf_b).astype(jnp.bfloat16)
    diagonal_ones = jnp.eye(ATOMS, dtype=jnp.float32)
    pair_live = live_own[:, None] * live_near[None, :] * (1.0 - self_flag * diagonal_ones)
    envelope = jnp.where(distance < cutoff, 0.5 * (jnp.cos(math.pi * distance / cutoff) + 1.0), 0.0) * pair_live
    kernel = (jnp.dot(hidden, filt_w, preferred_element_type=jnp.float32) + filt_b) * envelope.reshape(ATOMS * ATOMS, 1)
    kernel = kernel.astype(jnp.bfloat16).astype(jnp.float32).reshape(ATOMS, ATOMS, F)
    to_own = lax.optimization_barrier(jnp.sum(kernel * value_near[None, :, :], axis=1))
    to_near = lax.optimization_barrier(jnp.sum(kernel * value_own[:, None, :], axis=0))
    return (to_own, to_near)

def tile_group(items, offset_vec, self_flag, weights):
    mapped = jax.vmap(pair_tile, in_axes=(0, 0, 0, 0, 0, 0, None, None, None))
    return mapped(items[0], items[1], items[2], items[3], items[4], items[5], offset_vec, self_flag, weights)

def reference(features, positions, counts, rbf_weight, rbf_bias, filter_weight, filter_bias, input_weight, output_weight, output_bias, final_weight, final_bias):
    grid = counts.shape
    total = grid[0] * grid[1] * grid[2]
    group = math.gcd(total, 16)
    slots = jnp.arange(ATOMS, dtype=jnp.int32)
    live = (slots < counts[..., None]).astype(jnp.float32)
    state = features
    for layer in range(BLOCKS):
        weights = (rbf_weight[layer], rbf_bias[layer], filter_weight[layer], filter_bias[layer])
        values = jnp.dot(state.reshape(-1, F), input_weight[layer], precision=lax.Precision.HIGHEST, preferred_element_type=jnp.float32).reshape(state.shape)
        gathered = jnp.zeros(state.shape, jnp.float32)
        for offset in half_offsets():
            moved = (-offset[0], -offset[1], -offset[2])
            near_pos = jnp.roll(positions, moved, axis=(0, 1, 2))
            near_live = jnp.roll(live, moved, axis=(0, 1, 2))
            near_values = jnp.roll(values, moved, axis=(0, 1, 2))
            items = (positions.reshape(-1, group, 3, ATOMS), live.reshape(-1, group, ATOMS), values.reshape(-1, group, ATOMS, F), near_pos.reshape(-1, group, 3, ATOMS), near_live.reshape(-1, group, ATOMS), near_values.reshape(-1, group, ATOMS, F))
            self_flag = 1.0 if offset == (0, 0, 0) else 0.0
            offset_vec = jnp.array(offset, dtype=jnp.float32)
            to_own, to_near = lax.map(partial(tile_group, offset_vec=offset_vec, self_flag=self_flag, weights=weights), items)
            gathered = gathered + to_own.reshape(state.shape)
            if offset != (0, 0, 0):
                gathered = gathered + jnp.roll(to_near.reshape(state.shape), offset, axis=(0, 1, 2))
        gathered = gathered * scale_sum
        mixed = shifted_softplus(jnp.dot(gathered.reshape(-1, F), output_weight[layer], precision=lax.Precision.HIGHEST, preferred_element_type=jnp.float32) + output_bias[layer])
        update = jnp.dot(mixed, final_weight[layer], precision=lax.Precision.HIGHEST, preferred_element_type=jnp.float32) + final_bias[layer]
        state = (state + update.reshape(state.shape)) * live[..., None]
    return state
```

```python
import functools
import math

import jax
import jax.numpy as jnp
import numpy as np
from jax import lax
from jax.experimental import pallas as pl
from jax.experimental.pallas import tpu as pltpu
from jax.sharding import PartitionSpec as P

F = 128
RBF = 64
ATOMS = 64
BLOCKS = 2

cell_edge = 8.0
cutoff = 5.0
gamma = 10.0
scale_sum = 0.125

ROWS = 36 * ATOMS
PACKS = ROWS // F
SLOTS = 512
TILE = 256
HI = lax.Precision.HIGHEST


def shifted(x, axis, by):
    peers = lax.axis_size(axis)
    return lax.ppermute(x, axis, [(i, (i + by) % peers) for i in range(peers)])


def softplus(v):
    return jnp.maximum(v, 0.0) + jnp.log(1.0 + jnp.exp(-jnp.abs(v))) - math.log(2.0)


def region_table():
    table = np.zeros((8, ROWS), np.float32)
    for dx in range(3):
        for dy in range(3):
            for k, z in enumerate((0, 1, 2, -1)):
                q = (dx * 3 + dy) * 4 + k
                at = slice(q * ATOMS, (q + 1) * ATOMS)
                table[0, at] = cell_edge * (dx - 1)
                table[1, at] = cell_edge * (dy - 1)
                table[2, at] = cell_edge * z
                table[3, at] = np.arange(ATOMS) + 1 if q == 16 else 100
                table[4, at] = np.arange(ATOMS) + 1 if q == 17 else 100
    return table


def scan_table():
    lower = np.triu(np.ones((F, F), np.float32))
    return np.concatenate([lower, np.ones((F, F), np.float32)], axis=1)


def iota(shape, dim):
    return lax.broadcasted_iota(jnp.int32, shape, dim)


def dot(a, b):
    return jnp.dot(a, b, preferred_element_type=jnp.float32)


def pieces3(x):
    a = x.astype(jnp.bfloat16)
    r = x - a.astype(jnp.float32)
    b = r.astype(jnp.bfloat16)
    c = (r - b.astype(jnp.float32)).astype(jnp.bfloat16)
    return a, b, c


def block_kernel(
    packs_ref, vals_ref, state_ref, table_ref, scan_ref,
    rw_ref, rb_ref, fw_ref, fb_ref, ow_ref, ob_ref, nw_ref, nb_ref, iw_ref,
    out_ref, next_ref,
    vhl, coords, slot_of, oh1, near, w3, orep, rrep, lanes, acc,
):
    for g in range(PACKS):
        coords[:, g * F:(g + 1) * F] = packs_ref[g]

    @pl.loop(0, ROWS // 256)
    def _(k):
        at = pl.ds(pl.multiple_of(k * 256, 256), 256)
        v = vals_ref[at, :]
        top = v.astype(jnp.bfloat16)
        vhl[at, 0:F] = top
        vhl[at, F:2 * F] = (v - top.astype(jnp.float32)).astype(jnp.bfloat16)

    acc[...] = jnp.zeros_like(acc)

    @pl.loop(0, 2)
    def _(c):
        base = c * ATOMS
        pick = iota((ATOMS, F), 1) == iota((ATOMS, F), 0) + base
        own = packs_ref[8]

        def column(r):
            return jnp.sum(jnp.where(pick, own[r:r + 1, :], 0.0), axis=1, keepdims=True)

        ox, oy, oz, olive = column(0), column(1), column(2), column(3)
        zshift = cell_edge * c.astype(jnp.float32)

        def placed(at):
            px = coords[0:1, at] + table_ref[0:1, at]
            py = coords[1:2, at] + table_ref[1:2, at]
            pz = coords[2:3, at] + (table_ref[2:3, at] - zshift)
            return px, py, pz

        anys = []
        for k in range(PACKS):
            at = slice(k * F, (k + 1) * F)
            px, py, pz = placed(at)
            dx, dy, dz = px - ox, py - oy, pz - oz
            near_enough = jnp.where(dx * dx + dy * dy + dz * dz < cutoff * cutoff, olive, 0.0)
            hit = jnp.max(near_enough, axis=0, keepdims=True) * coords[3:4, at]
            anys.append(jnp.broadcast_to(hit, (8, F)))
        stacked = jnp.concatenate(anys, axis=0)
        scanned = dot(stacked.astype(jnp.bfloat16), scan_ref[...])
        carry = jnp.zeros((8, F), jnp.float32)
        for k in range(PACKS):
            part = scanned[k * 8:(k + 1) * 8]
            slot_of[:, k * F:(k + 1) * F] = jnp.where(
                anys[k] > 0.5, carry + part[:, 0:F] - 1.0, -1.0
            )
            carry = carry + part[:, F:2 * F]
        found = jnp.max(carry).astype(jnp.int32)

        @pl.loop(0, (found + SLOTS - 1) // SLOTS)
        def _(h):
            first = h * SLOTS
            want = (iota((SLOTS, F), 0) + first).astype(jnp.float32)
            for k in range(PACKS):
                at = slice(k * F, (k + 1) * F)
                oh1[:, at] = jnp.where(slot_of[0:1, at] == want, 1.0, 0.0).astype(jnp.bfloat16)
            near[...] = dot(oh1[...], vhl[...]).astype(jnp.bfloat16)
            px, py, pz = placed(slice(0, ROWS))
            ids = table_ref[pl.ds(3 + c, 1), :].astype(jnp.bfloat16)
            rows = [*pieces3(px), *pieces3(py), *pieces3(pz), ids]
            rows = jnp.concatenate(
                [r.astype(jnp.float32) for r in rows] + [jnp.zeros((6, ROWS), jnp.float32)], axis=0
            ).astype(jnp.bfloat16)
            packed = lax.dot_general(
                rows, oh1[...], (((1,), (1,)), ((), ())), preferred_element_type=jnp.float32
            )
            cx = packed[0:1] + packed[1:2] + packed[2:3]
            cy = packed[3:4] + packed[4:5] + packed[5:6]
            cz = packed[6:7] + packed[7:8] + packed[8:9]
            cid = packed[9:10]
            dx, dy, dz = cx - ox, cy - oy, cz - oz
            dist = jnp.sqrt(dx * dx + dy * dy + dz * dz)
            me = (iota((ATOMS, SLOTS), 0) + 1).astype(jnp.float32)
            keep = (dist < cutoff) & (cid > 0.5) & (cid != me) & (olive > 0.5)
            ones = jnp.where(keep, 1.0, 0.0)
            envelope = jnp.where(
                keep, 0.5 * (jnp.cos(math.pi * dist / cutoff) + 1.0), 0.0
            )
            dist = jnp.where(keep, dist, 0.0)
            parts = jnp.concatenate(
                [ones[:, k * F:(k + 1) * F] for k in range(SLOTS // F)], axis=0
            ).astype(jnp.bfloat16)
            scanned = dot(parts, scan_ref[...])
            run = jnp.zeros((ATOMS, F), jnp.float32)
            ranks = []
            for k in range(SLOTS // F):
                part = scanned[k * ATOMS:(k + 1) * ATOMS]
                ranks.append(run + part[:, 0:F])
                run = run + part[:, F:2 * F]
            strict = jnp.where(
                iota((ATOMS, ATOMS), 0) > iota((ATOMS, ATOMS), 1), 1.0, 0.0
            )
            offset = jnp.dot(strict, run, precision=HI, preferred_element_type=jnp.float32)
            orep[...] = offset
            rrep[...] = run
            pairs = jnp.max(offset + run).astype(jnp.int32)
            offset_all = jnp.concatenate([offset] * (SLOTS // F), axis=1)
            index = jnp.where(keep, offset_all + jnp.concatenate(ranks, axis=1), 0.0).astype(
                jnp.int32
            )
            w3[0:64, 0:SLOTS] = (index & ~16383).astype(jnp.float32).astype(jnp.bfloat16)
            w3[64:128, 0:SLOTS] = (index & (127 * 128)).astype(jnp.float32).astype(jnp.bfloat16)
            w3[128:192, 0:SLOTS] = (index & 127).astype(jnp.float32).astype(jnp.bfloat16)
            for n, parts3 in enumerate((pieces3(dist), pieces3(envelope))):
                for r, piece in enumerate(parts3):
                    w3[r * 64:(r + 1) * 64, (n + 1) * SLOTS:(n + 2) * SLOTS] = piece
            w3[192:256, :] = jnp.zeros((64, 3 * SLOTS), jnp.bfloat16)
            spread = ((iota((ATOMS, 2 * F), 1) & 63) == iota((ATOMS, 2 * F), 0)) & (
                iota((ATOMS, 2 * F), 1) < 192
            )
            two = jnp.concatenate([offset, offset], axis=1)
            low = jnp.sum(jnp.where(spread, two, 0.0), axis=0, keepdims=True)
            two = jnp.concatenate([run, run], axis=1)
            count = jnp.sum(jnp.where(spread, two, 0.0), axis=0, keepdims=True)
            lanes[0:1, :] = low
            lanes[1:2, :] = low + count

            @pl.loop(0, (pairs + TILE - 1) // TILE)
            def _(t):
                start = (t * TILE).astype(jnp.float32)
                p = iota((TILE, 2 * F), 0).astype(jnp.float32) + start
                member = jnp.where((lanes[0:1, :] <= p) & (p < lanes[1:2, :]), 1.0, 0.0)
                member = member.astype(jnp.bfloat16)
                p1 = iota((TILE, SLOTS), 0).astype(jnp.float32) + (start + 1.0)
                hot = dot(member, w3[:, 0:SLOTS]) == p1
                d = jnp.sum(
                    jnp.where(hot, dot(member, w3[:, SLOTS:2 * SLOTS]), 0.0), axis=1, keepdims=True
                )
                e = jnp.sum(
                    jnp.where(hot, dot(member, w3[:, 2 * SLOTS:3 * SLOTS]), 0.0),
                    axis=1,
                    keepdims=True,
                )
                onehot = jnp.where(hot, 1.0, 0.0).astype(jnp.bfloat16)
                got = dot(onehot, near[...])
                got = got[:, 0:F] + got[:, F:2 * F]
                centres = iota((TILE, RBF), 1).astype(jnp.float32) * (cutoff / (RBF - 1))
                apart = d - centres
                radial = jnp.exp(-gamma * apart * apart).astype(jnp.bfloat16)
                hidden = softplus(dot(radial, rw_ref[...]) + rb_ref[...]).astype(jnp.bfloat16)
                kern = ((dot(hidden, fw_ref[...]) + fb_ref[...]) * e).astype(jnp.bfloat16)
                prod = kern.astype(jnp.float32) * got
                top = prod.astype(jnp.bfloat16)
                rest = (prod - top.astype(jnp.float32)).astype(jnp.bfloat16)
                pl_ = iota((ATOMS, TILE), 1).astype(jnp.float32) + start
                lo = jnp.concatenate([orep[...], orep[...]], axis=1)
                hi = lo + jnp.concatenate([rrep[...], rrep[...]], axis=1)
                back = jnp.where((lo <= pl_) & (pl_ < hi), 1.0, 0.0).astype(jnp.bfloat16)
                summed = dot(back, jnp.concatenate([top, rest], axis=1))
                at = pl.ds(pl.multiple_of(base, ATOMS), ATOMS)
                acc[at, :] += summed[:, 0:F] + summed[:, F:2 * F]

    def dense(x, w):
        return jnp.dot(x, w, precision=HI, preferred_element_type=jnp.float32)

    mixed = softplus(dense(acc[...] * scale_sum, ow_ref[...]) + ob_ref[...])
    update = dense(mixed, nw_ref[...]) + nb_ref[...]
    own = packs_ref[8]
    diag = iota((F, F), 0) == iota((F, F), 1)
    live = jnp.sum(jnp.where(diag, own[3:4, :], 0.0), axis=1, keepdims=True)
    state = (state_ref[...] + update) * live
    out_ref[...] = state
    next_ref[...] = dense(state, iw_ref[...])


def run_block(packs, vals, state, table, scan, *weights):
    return pl.pallas_call(
        block_kernel,
        out_shape=(
            jax.ShapeDtypeStruct((2 * ATOMS, F), jnp.float32),
            jax.ShapeDtypeStruct((2 * ATOMS, F), jnp.float32),
        ),
        in_specs=[pl.BlockSpec(memory_space=pltpu.VMEM)] * 14,
        out_specs=[pl.BlockSpec(memory_space=pltpu.VMEM)] * 2,
        scratch_shapes=[
            pltpu.VMEM((ROWS, 2 * F), jnp.bfloat16),
            pltpu.VMEM((8, ROWS), jnp.float32),
            pltpu.VMEM((8, ROWS), jnp.float32),
            pltpu.VMEM((SLOTS, ROWS), jnp.bfloat16),
            pltpu.VMEM((SLOTS, 2 * F), jnp.bfloat16),
            pltpu.VMEM((256, 3 * SLOTS), jnp.bfloat16),
            pltpu.VMEM((ATOMS, F), jnp.float32),
            pltpu.VMEM((ATOMS, F), jnp.float32),
            pltpu.VMEM((8, 2 * F), jnp.float32),
            pltpu.VMEM((2 * ATOMS, F), jnp.float32),
        ],
        compiler_params=pltpu.CompilerParams(vmem_limit_bytes=48 << 20),
    )(packs, vals, state, table, scan, *weights)


def halo_values(v):
    v = v.reshape(2, ATOMS, F)
    v = jnp.stack([shifted(v, "gy", 1), v, shifted(v, "gy", -1)])
    left, right = shifted(v[:, 1], "gz", 1), shifted(v[:, 0], "gz", -1)
    v = jnp.concatenate([v, right[:, None], left[:, None]], axis=1)
    v = jnp.stack([shifted(v, "gx", 1), v, shifted(v, "gx", -1)])
    return v.reshape(ROWS, F)


def halo_packs(p):
    p = jnp.stack([shifted(p, "gy", 1), p, shifted(p, "gy", -1)])
    left, right = shifted(p, "gz", 1), shifted(p, "gz", -1)
    lower = lax.broadcasted_iota(jnp.int32, p.shape, 2) < ATOMS
    p = jnp.stack([p, jnp.where(lower, right, left)], axis=1)
    p = jnp.stack([shifted(p, "gx", 1), p, shifted(p, "gx", -1)])
    return p.reshape(PACKS, 8, F)


def shards(
    features,
    positions,
    counts,
    rbf_weight,
    rbf_bias,
    filter_weight,
    filter_bias,
    input_weight,
    output_weight,
    output_bias,
    final_weight,
    final_bias,
):
    state = features.reshape(2 * ATOMS, F)
    slots = jnp.arange(ATOMS, dtype=jnp.int32)
    live = (slots[None, :] < counts.reshape(2, 1)).astype(jnp.float32)
    pack = jnp.concatenate([positions.reshape(2, 3, ATOMS), live[:, None, :]], axis=1)
    pack = jnp.transpose(pack, (1, 0, 2)).reshape(4, F)
    pack = jnp.concatenate([pack, jnp.zeros((4, F), jnp.float32)], axis=0)
    packs = halo_packs(pack)
    table = jnp.asarray(region_table())
    scan = jnp.asarray(scan_table(), dtype=jnp.bfloat16)
    values = jnp.dot(state, input_weight[0], precision=HI, preferred_element_type=jnp.float32)
    for b in range(BLOCKS):
        state, values = run_block(
            packs,
            halo_values(values),
            state,
            table,
            scan,
            rbf_weight[b],
            rbf_bias[b][None],
            filter_weight[b],
            filter_bias[b][None],
            output_weight[b],
            output_bias[b][None],
            final_weight[b],
            final_bias[b][None],
            input_weight[(b + 1) % BLOCKS],
        )
    return state.reshape(features.shape)


def solution(mesh):
    cells = P("gx", "gy", "gz", None, None)
    placed = (cells, cells, P("gx", "gy", "gz")) + (P(),) * 9
    return jax.shard_map(
        shards, mesh=mesh, in_specs=placed, out_specs=cells, check_vma=False
    )
```

```python
import math

import jax
import jax.numpy as jnp
import numpy as np
from jax import lax
from jax.experimental import pallas as pl
from jax.experimental.pallas import tpu as pltpu
from jax.sharding import PartitionSpec as P

F = 128
RBF = 64
ATOMS = 64
BLOCKS = 2

cell_edge = 8.0
cutoff = 5.0
gamma = 10.0
scale_sum = 0.125

ROWS = 36 * ATOMS
PACKS = ROWS // F
SLOTS = 512
TILE = 256
CAP = 48
HI = lax.Precision.HIGHEST
VMEM = pl.BlockSpec(memory_space=pltpu.VMEM)
ANY = pl.BlockSpec(memory_space=pl.ANY)
SMEM = pl.BlockSpec(memory_space=pltpu.SMEM)


def softplus(v):
    return jnp.maximum(v, 0.0) + jnp.log(1.0 + jnp.exp(-jnp.abs(v))) - math.log(2.0)


def region_table():
    table = np.zeros((8, ROWS), np.float32)
    for dx in range(3):
        for dy in range(3):
            for k, z in enumerate((0, 1, 2, -1)):
                q = (dx * 3 + dy) * 4 + k
                at = slice(q * ATOMS, (q + 1) * ATOMS)
                table[0, at] = cell_edge * (dx - 1)
                table[1, at] = cell_edge * (dy - 1)
                table[2, at] = cell_edge * z
                table[3, at] = np.arange(ATOMS) + 1 if q == 16 else 100
                table[4, at] = np.arange(ATOMS) + 1 if q == 17 else 100
    return table


def iota(shape, dim):
    return lax.broadcasted_iota(jnp.int32, shape, dim)


def dot(a, b):
    return jnp.dot(a, b, preferred_element_type=jnp.float32)


def pieces3(x):
    a = x.astype(jnp.bfloat16)
    r = x - a.astype(jnp.float32)
    b = r.astype(jnp.bfloat16)
    c = (r - b.astype(jnp.float32)).astype(jnp.bfloat16)
    return a, b, c


def slow_cells(
    b, coords, table_ref, vhl, rw_ref, rb_ref, fw_ref, fb_ref,
    scan_ref, slot_of, oh1, near, w3, orep, rrep, lanes, acc,
):
    acc[...] = jnp.zeros_like(acc)

    @pl.loop(0, 2)
    def _(c):
        base = c * ATOMS
        pick = iota((ATOMS, F), 1) == iota((ATOMS, F), 0) + base
        own = coords[:, 8 * F:9 * F]

        def column(r):
            return jnp.sum(jnp.where(pick, own[r:r + 1, :], 0.0), axis=1, keepdims=True)

        ox, oy, oz, olive = column(0), column(1), column(2), column(3)
        zshift = cell_edge * c.astype(jnp.float32)

        def placed(at):
            px = coords[0:1, at] + table_ref[0:1, at]
            py = coords[1:2, at] + table_ref[1:2, at]
            pz = coords[2:3, at] + (table_ref[2:3, at] - zshift)
            return px, py, pz

        anys = []
        for k in range(PACKS):
            at = slice(k * F, (k + 1) * F)
            px, py, pz = placed(at)
            dx, dy, dz = px - ox, py - oy, pz - oz
            near_enough = jnp.where(dx * dx + dy * dy + dz * dz < cutoff * cutoff, olive, 0.0)
            hit = jnp.max(near_enough, axis=0, keepdims=True) * coords[3:4, at]
            anys.append(jnp.broadcast_to(hit, (8, F)))
        stacked = jnp.concatenate(anys, axis=0)
        scanned = dot(stacked.astype(jnp.bfloat16), scan_ref[...])
        carry = jnp.zeros((8, F), jnp.float32)
        for k in range(PACKS):
            part = scanned[k * 8:(k + 1) * 8]
            slot_of[:, k * F:(k + 1) * F] = jnp.where(
                anys[k] > 0.5, carry + part[:, 0:F] - 1.0, -1.0
            )
            carry = carry + part[:, F:2 * F]
        found = jnp.max(carry).astype(jnp.int32)

        @pl.loop(0, (found + SLOTS - 1) // SLOTS)
        def _(h):
            first = h * SLOTS
            want = (iota((SLOTS, F), 0) + first).astype(jnp.float32)
            for k in range(PACKS):
                at = slice(k * F, (k + 1) * F)
                oh1[:, at] = jnp.where(slot_of[0:1, at] == want, 1.0, 0.0).astype(jnp.bfloat16)
            near[...] = dot(oh1[...], vhl[...]).astype(jnp.bfloat16)
            px, py, pz = placed(slice(0, ROWS))
            ids = table_ref[pl.ds(3 + c, 1), :].astype(jnp.bfloat16)
            rows = [*pieces3(px), *pieces3(py), *pieces3(pz), ids]
            rows = jnp.concatenate(
                [r.astype(jnp.float32) for r in rows] + [jnp.zeros((6, ROWS), jnp.float32)], axis=0
            ).astype(jnp.bfloat16)
            packed = lax.dot_general(
                rows, oh1[...], (((1,), (1,)), ((), ())), preferred_element_type=jnp.float32
            )
            cx = packed[0:1] + packed[1:2] + packed[2:3]
            cy = packed[3:4] + packed[4:5] + packed[5:6]
            cz = packed[6:7] + packed[7:8] + packed[8:9]
            cid = packed[9:10]
            dx, dy, dz = cx - ox, cy - oy, cz - oz
            dist = jnp.sqrt(dx * dx + dy * dy + dz * dz)
            me = (iota((ATOMS, SLOTS), 0) + 1).astype(jnp.float32)
            keep = (dist < cutoff) & (cid > 0.5) & (cid != me) & (olive > 0.5)
            ones = jnp.where(keep, 1.0, 0.0)
            envelope = jnp.where(
                keep, 0.5 * (jnp.cos(math.pi * dist / cutoff) + 1.0), 0.0
            )
            dist = jnp.where(keep, dist, 0.0)
            parts = jnp.concatenate(
                [ones[:, k * F:(k + 1) * F] for k in range(SLOTS // F)], axis=0
            ).astype(jnp.bfloat16)
            scanned = dot(parts, scan_ref[...])
            run = jnp.zeros((ATOMS, F), jnp.float32)
            ranks = []
            for k in range(SLOTS // F):
                part = scanned[k * ATOMS:(k + 1) * ATOMS]
                ranks.append(run + part[:, 0:F])
                run = run + part[:, F:2 * F]
            strict = jnp.where(
                iota((ATOMS, ATOMS), 0) > iota((ATOMS, ATOMS), 1), 1.0, 0.0
            )
            offset = jnp.dot(strict, run, precision=HI, preferred_element_type=jnp.float32)
            orep[...] = offset
            rrep[...] = run
            pairs = jnp.max(offset + run).astype(jnp.int32)
            offset_all = jnp.concatenate([offset] * (SLOTS // F), axis=1)
            index = jnp.where(keep, offset_all + jnp.concatenate(ranks, axis=1), 0.0).astype(
                jnp.int32
            )
            w3[0:64, 0:SLOTS] = (index & ~16383).astype(jnp.float32).astype(jnp.bfloat16)
            w3[64:128, 0:SLOTS] = (index & (127 * 128)).astype(jnp.float32).astype(jnp.bfloat16)
            w3[128:192, 0:SLOTS] = (index & 127).astype(jnp.float32).astype(jnp.bfloat16)
            for n, parts3 in enumerate((pieces3(dist), pieces3(envelope))):
                for r, piece in enumerate(parts3):
                    w3[r * 64:(r + 1) * 64, (n + 1) * SLOTS:(n + 2) * SLOTS] = piece
            w3[192:256, :] = jnp.zeros((64, 3 * SLOTS), jnp.bfloat16)
            spread = ((iota((ATOMS, 2 * F), 1) & 63) == iota((ATOMS, 2 * F), 0)) & (
                iota((ATOMS, 2 * F), 1) < 192
            )
            two = jnp.concatenate([offset, offset], axis=1)
            low = jnp.sum(jnp.where(spread, two, 0.0), axis=0, keepdims=True)
            two = jnp.concatenate([run, run], axis=1)
            count = jnp.sum(jnp.where(spread, two, 0.0), axis=0, keepdims=True)
            lanes[0:1, :] = low
            lanes[1:2, :] = low + count

            @pl.loop(0, (pairs + TILE - 1) // TILE)
            def _(t):
                start = (t * TILE).astype(jnp.float32)
                p = iota((TILE, 2 * F), 0).astype(jnp.float32) + start
                member = jnp.where((lanes[0:1, :] <= p) & (p < lanes[1:2, :]), 1.0, 0.0)
                member = member.astype(jnp.bfloat16)
                p1 = iota((TILE, SLOTS), 0).astype(jnp.float32) + (start + 1.0)
                hot = dot(member, w3[:, 0:SLOTS]) == p1
                d = jnp.sum(
                    jnp.where(hot, dot(member, w3[:, SLOTS:2 * SLOTS]), 0.0), axis=1, keepdims=True
                )
                e = jnp.sum(
                    jnp.where(hot, dot(member, w3[:, 2 * SLOTS:3 * SLOTS]), 0.0),
                    axis=1,
                    keepdims=True,
                )
                onehot = jnp.where(hot, 1.0, 0.0).astype(jnp.bfloat16)
                got = dot(onehot, near[...])
                got = got[:, 0:F] + got[:, F:2 * F]
                centres = iota((TILE, RBF), 1).astype(jnp.float32) * (cutoff / (RBF - 1))
                apart = d - centres
                radial = jnp.exp(-gamma * apart * apart).astype(jnp.bfloat16)
                hidden = softplus(dot(radial, rw_ref[b]) + rb_ref[b:b + 1]).astype(jnp.bfloat16)
                kern = ((dot(hidden, fw_ref[b]) + fb_ref[b:b + 1]) * e).astype(jnp.bfloat16)
                prod = kern.astype(jnp.float32) * got
                top = prod.astype(jnp.bfloat16)
                rest = (prod - top.astype(jnp.float32)).astype(jnp.bfloat16)
                pl_ = iota((ATOMS, TILE), 1).astype(jnp.float32) + start
                lo = jnp.concatenate([orep[...], orep[...]], axis=1)
                hi = lo + jnp.concatenate([rrep[...], rrep[...]], axis=1)
                back = jnp.where((lo <= pl_) & (pl_ < hi), 1.0, 0.0).astype(jnp.bfloat16)
                summed = dot(back, jnp.concatenate([top, rest], axis=1))
                at = pl.ds(pl.multiple_of(base, ATOMS), ATOMS)
                acc[at, :] += summed[:, 0:F] + summed[:, F:2 * F]


def dense(x, w):
    return jnp.dot(x, w, precision=HI, preferred_element_type=jnp.float32)


def region_rows(dx, dy, k, cells):
    return pl.ds((((dx + 1) * 3 + dy + 1) * 4 + k) * ATOMS, cells * ATOMS)


def neighbours():
    return [
        (ox, oy, oz)
        for ox in (-1, 0, 1)
        for oy in (-1, 0, 1)
        for oz in (-1, 0, 1)
        if (ox, oy, oz) != (0, 0, 0)
    ]


def device_at(offset):
    return tuple(
        lax.rem(lax.axis_index(a) + (o + lax.axis_size(a)), lax.axis_size(a))
        for a, o in zip(("gx", "gy", "gz"), offset)
    )


def greet(offsets):
    barrier = pltpu.get_barrier_semaphore()
    for o in offsets:
        pl.semaphore_signal(
            barrier, inc=1, device_id=device_at(o), device_id_type=pl.DeviceIdType.MESH
        )
    pl.semaphore_wait(barrier, len(offsets))


FACES = [(0, 1, 0), (0, -1, 0), (0, 0, 1), (0, 0, -1), (1, 0, 0), (-1, 0, 0)]


def spread_values(vals, region, ssem, rsem):
    copies = {}

    def send(name, src, dst, to):
        n = len(copies)
        copies[name] = pltpu.make_async_remote_copy(
            src_ref=src,
            dst_ref=region.at[dst],
            send_sem=ssem.at[n],
            recv_sem=rsem.at[n],
            device_id=device_at(to),
            device_id_type=pl.DeviceIdType.MESH,
        )
        copies[name].start()

    def cells(dy, k, n):
        if dy == 0 and k < 2:
            return vals.at[pl.ds(k * ATOMS, n * ATOMS)]
        return region.at[region_rows(0, dy, k, n)]

    def send_z(dy):
        send(("z", dy, 3), cells(dy, 1, 1), region_rows(0, dy, 3, 1), (0, 0, 1))
        send(("z", dy, 2), cells(dy, 0, 1), region_rows(0, dy, 2, 1), (0, 0, -1))

    def send_x(dy, k):
        send(("x", dy, k, 1), cells(dy, k, 2), region_rows(-1, dy, k, 2), (1, 0, 0))
        send(("x", dy, k, -1), cells(dy, k, 2), region_rows(1, dy, k, 2), (-1, 0, 0))

    send(("y", -1), cells(0, 0, 2), region_rows(0, -1, 0, 2), (0, 1, 0))
    send(("y", 1), cells(0, 0, 2), region_rows(0, 1, 0, 2), (0, -1, 0))
    send_z(0)
    send_x(0, 0)
    region[region_rows(0, 0, 0, 2), :] = vals[...]
    for k in (2, 3):
        copies["z", 0, k].wait_recv()
    send_x(0, 2)
    for dy in (-1, 1):
        copies["y", dy].wait_recv()
        send_z(dy)
        send_x(dy, 0)
    for dy in (-1, 1):
        for k in (2, 3):
            copies["z", dy, k].wait_recv()
        send_x(dy, 2)
    for name, copy in copies.items():
        if name[0] == "x":
            copy.wait_recv()
    for copy in copies.values():
        copy.wait_send()


def first_comm(
    counts_ref, state_ref, pos_ref, iw_ref, region, packs, vals, pack, ssem, rsem, psend, precv
):
    live = [
        jnp.where(iota((1, ATOMS), 1) < counts_ref[c], 1.0, 0.0) for c in range(2)
    ]
    rows = [
        jnp.concatenate([pos_ref[c], live[c], jnp.zeros((4, ATOMS), jnp.float32)], axis=0)
        for c in range(2)
    ]
    pack[...] = jnp.concatenate(rows, axis=1)
    vals[...] = dense(state_ref[...], iw_ref[0])
    greet(neighbours())
    copies = []
    for n, (ox, oy, oz) in enumerate(neighbours()):
        slot = (1 - ox) * 9 + (1 - oy) * 3 + (1 - oz)
        copies.append(
            pltpu.make_async_remote_copy(
                src_ref=pack,
                dst_ref=packs.at[slot],
                send_sem=psend.at[n],
                recv_sem=precv.at[n],
                device_id=device_at((ox, oy, oz)),
                device_id_type=pl.DeviceIdType.MESH,
            )
        )
        copies[-1].start()
    packs[13] = pack[...]
    spread_values(vals, region, ssem, rsem)
    for copy in copies:
        copy.wait_recv()
    for copy in copies:
        copy.wait_send()


def later_comm(vals_ref, region, ssem, rsem):
    greet(FACES)
    spread_values(vals_ref, region, ssem, rsem)


REGION = jax.ShapeDtypeStruct((ROWS, F), jnp.float32)
PACKED = jax.ShapeDtypeStruct((27, 8, F), jnp.float32)


def start_halo(counts, state, positions, input_weight):
    return pl.pallas_call(
        first_comm,
        out_shape=(REGION, PACKED),
        in_specs=[SMEM, VMEM, VMEM, VMEM],
        out_specs=(VMEM, VMEM),
        scratch_shapes=[
            pltpu.VMEM((2 * ATOMS, F), jnp.float32),
            pltpu.VMEM((8, F), jnp.float32),
            pltpu.SemaphoreType.DMA((20,)),
            pltpu.SemaphoreType.DMA((20,)),
            pltpu.SemaphoreType.DMA((26,)),
            pltpu.SemaphoreType.DMA((26,)),
        ],
        compiler_params=pltpu.CompilerParams(collective_id=0, has_side_effects=True),
    )(counts, state, positions, input_weight)


def later_halo(vals):
    return pl.pallas_call(
        later_comm,
        out_shape=REGION,
        in_specs=[VMEM],
        out_specs=VMEM,
        scratch_shapes=[pltpu.SemaphoreType.DMA((20,)), pltpu.SemaphoreType.DMA((20,))],
        compiler_params=pltpu.CompilerParams(collective_id=1, has_side_effects=True),
    )(vals)


def split_values(region, vhl):
    @pl.loop(0, ROWS // 256)
    def _(k):
        at = pl.ds(pl.multiple_of(k * 256, 256), 256)
        v = region[at, :]
        top = v.astype(jnp.bfloat16)
        vhl[at, 0:F] = top
        vhl[at, F:2 * F] = (v - top.astype(jnp.float32)).astype(jnp.bfloat16)


def place_packs(packs, coords):
    lower = iota((8, F), 1) < ATOMS
    for q in range(9):
        coords[:, 2 * q * F:(2 * q + 1) * F] = packs[3 * q + 1]
        coords[:, (2 * q + 1) * F:(2 * q + 2) * F] = jnp.where(
            lower, packs[3 * q + 2], packs[3 * q]
        )


def fill_scan(scan):
    upper = iota((F, F), 0) <= iota((F, F), 1)
    scan[:, 0:F] = jnp.where(upper, 1.0, 0.0).astype(jnp.bfloat16)
    scan[:, F:2 * F] = jnp.ones((F, F), jnp.bfloat16)


def pick_rows(slots, oh1, c):
    want = iota((SLOTS, F), 0).astype(jnp.float32)
    for k in range(PACKS):
        at = slice(k * F, (k + 1) * F)
        row = slots[pl.ds(8 * c, 1), at]
        oh1[:, at] = jnp.where(row == want, 1.0, 0.0).astype(jnp.bfloat16)


def finish(b, coords, state_ref, acc, ow, ob, nw, nb):
    mixed = softplus(dense(acc[...] * scale_sum, ow[b]) + ob[b:b + 1])
    update = dense(mixed, nw[b]) + nb[b:b + 1]
    diag = iota((F, F), 0) == iota((F, F), 1)
    live = jnp.sum(jnp.where(diag, coords[3:4, 8 * F:9 * F], 0.0), axis=1, keepdims=True)
    return (state_ref[...] + update) * live


def add_pairs(onehot, kern, near, low, size, start):
    got = dot(onehot, near)
    got = got[:, 0:F] + got[:, F:2 * F]
    prod = kern.astype(jnp.float32) * got
    top = prod.astype(jnp.bfloat16)
    rest = (prod - top.astype(jnp.float32)).astype(jnp.bfloat16)
    p = iota((ATOMS, TILE), 1).astype(jnp.float32) + start
    lo = jnp.concatenate([low, low], axis=1)
    hi = lo + jnp.concatenate([size, size], axis=1)
    back = jnp.where((lo <= p) & (p < hi), 1.0, 0.0).astype(jnp.bfloat16)
    summed = dot(back, jnp.concatenate([top, rest], axis=1))
    return summed[:, 0:F] + summed[:, F:2 * F]


def first_block(
    region, packs, state_ref, table_ref,
    rw, rb, fw, fb, ow, ob, nw, nb, iw,
    out_ref, next_ref, slots, orep2, rrep2, meta, oh_hbm, kern_hbm,
    vhl, coords, scan, oh1, near2, rank2, dist2, lanes2, acc, oh_all, kern_all,
    rw_both, fw_both, slot_s, w3, orep, rrep, lanes, osem, ksem,
):
    place_packs(packs, coords)
    split_values(region, vhl)
    fill_scan(scan)
    rw_both[:, 0:F] = rw[0]
    rw_both[:, F:2 * F] = rw[1]
    fw_both[...] = jnp.zeros_like(fw_both)
    fw_both[0:F, 0:F] = fw[0]
    fw_both[F:2 * F, F:2 * F] = fw[1]
    acc[...] = jnp.zeros_like(acc)

    @pl.loop(0, 2)
    def _(c):
        base = c * ATOMS
        pick = iota((ATOMS, F), 1) == iota((ATOMS, F), 0) + base
        own = coords[:, 8 * F:9 * F]

        def column(r):
            return jnp.sum(jnp.where(pick, own[r:r + 1, :], 0.0), axis=1, keepdims=True)

        ox, oy, oz, olive = column(0), column(1), column(2), column(3)
        zshift = cell_edge * c.astype(jnp.float32)

        def placed(at):
            px = coords[0:1, at] + table_ref[0:1, at]
            py = coords[1:2, at] + table_ref[1:2, at]
            pz = coords[2:3, at] + (table_ref[2:3, at] - zshift)
            return px, py, pz

        anys = []
        for k in range(PACKS):
            at = slice(k * F, (k + 1) * F)
            px, py, pz = placed(at)
            dx, dy, dz = px - ox, py - oy, pz - oz
            near_enough = jnp.where(dx * dx + dy * dy + dz * dz < cutoff * cutoff, olive, 0.0)
            hit = jnp.max(near_enough, axis=0, keepdims=True) * coords[3:4, at]
            anys.append(jnp.broadcast_to(hit, (8, F)))
        scanned = dot(jnp.concatenate(anys, axis=0).astype(jnp.bfloat16), scan[...])
        carry = jnp.zeros((8, F), jnp.float32)
        mine = pl.ds(pl.multiple_of(8 * c, 8), 8)
        for k in range(PACKS):
            part = scanned[k * 8:(k + 1) * 8]
            slots[mine, k * F:(k + 1) * F] = jnp.where(
                anys[k] > 0.5, carry + part[:, 0:F] - 1.0, -1.0
            )
            carry = carry + part[:, F:2 * F]
        meta[c] = jnp.max(carry).astype(jnp.int32)

        pick_rows(slots, oh1, c)
        near2[c] = dot(oh1[...], vhl[...]).astype(jnp.bfloat16)
        px, py, pz = placed(slice(0, ROWS))
        ids = table_ref[pl.ds(3 + c, 1), :].astype(jnp.bfloat16)
        rows = [*pieces3(px), *pieces3(py), *pieces3(pz), ids]
        rows = jnp.concatenate(
            [r.astype(jnp.float32) for r in rows] + [jnp.zeros((6, ROWS), jnp.float32)], axis=0
        ).astype(jnp.bfloat16)
        packed = lax.dot_general(
            rows, oh1[...], (((1,), (1,)), ((), ())), preferred_element_type=jnp.float32
        )
        cx = packed[0:1] + packed[1:2] + packed[2:3]
        cy = packed[3:4] + packed[4:5] + packed[5:6]
        cz = packed[6:7] + packed[7:8] + packed[8:9]
        cid = packed[9:10]
        dx, dy, dz = cx - ox, cy - oy, cz - oz
        dist = jnp.sqrt(dx * dx + dy * dy + dz * dz)
        me = (iota((ATOMS, SLOTS), 0) + 1).astype(jnp.float32)
        keep = (dist < cutoff) & (cid > 0.5) & (cid != me) & (olive > 0.5)
        ones = jnp.where(keep, 1.0, 0.0)
        envelope = jnp.where(keep, 0.5 * (jnp.cos(math.pi * dist / cutoff) + 1.0), 0.0)
        both = jnp.concatenate([jnp.where(keep, dist, 0.0), envelope], axis=0)
        for k in range(SLOTS // F):
            at = slice(k * F, (k + 1) * F)
            turned = both[:, at].T
            top = turned.astype(jnp.bfloat16)
            dist2[c, at, 0:F] = top
            dist2[c, at, F:2 * F] = (turned - top.astype(jnp.float32)).astype(jnp.bfloat16)
        parts = jnp.concatenate(
            [ones[:, k * F:(k + 1) * F] for k in range(SLOTS // F)], axis=0
        ).astype(jnp.bfloat16)
        scanned = dot(parts, scan[...])
        run = jnp.zeros((ATOMS, F), jnp.float32)
        ranks = []
        for k in range(SLOTS // F):
            part = scanned[k * ATOMS:(k + 1) * ATOMS]
            ranks.append(run + part[:, 0:F])
            run = run + part[:, F:2 * F]
        strict = jnp.where(iota((ATOMS, ATOMS), 0) > iota((ATOMS, ATOMS), 1), 1.0, 0.0)
        offset = jnp.dot(strict, run, precision=HI, preferred_element_type=jnp.float32)
        orep2[c] = offset
        rrep2[c] = run
        meta[2 + c] = jnp.max(offset + run).astype(jnp.int32)
        offset_all = jnp.concatenate([offset] * (SLOTS // F), axis=1)
        index = jnp.where(keep, offset_all + jnp.concatenate(ranks, axis=1), 0.0).astype(jnp.int32)
        rank2[c, 0:64, :] = (index & ~255).astype(jnp.float32).astype(jnp.bfloat16)
        rank2[c, 64:128, :] = (index & 255).astype(jnp.float32).astype(jnp.bfloat16)
        spread = (iota((ATOMS, F), 1) & 63) == iota((ATOMS, F), 0)
        low = jnp.sum(jnp.where(spread, offset, 0.0), axis=0, keepdims=True)
        count = jnp.sum(jnp.where(spread, run, 0.0), axis=0, keepdims=True)
        lanes2[c, 0:1, :] = low
        lanes2[c, 1:2, :] = low + count

    tiles0 = (meta[2] + TILE - 1) // TILE
    tiles = tiles0 + (meta[3] + TILE - 1) // TILE
    fits = (meta[0] <= SLOTS) & (meta[1] <= SLOTS) & (tiles <= CAP)
    meta[4] = tiles0
    meta[5] = jnp.where(fits, tiles, 0)
    meta[6] = jnp.where(fits, 0, 1)
    meta[7] = 0

    def copies(t):
        at = pl.ds(pl.multiple_of(t * TILE, TILE), TILE)
        return (
            pltpu.make_async_copy(oh_all.at[at], oh_hbm.at[at], osem.at[t]),
            pltpu.make_async_copy(kern_all.at[at], kern_hbm.at[at], ksem.at[t]),
        )

    @pl.when(fits)
    def _():
        @pl.loop(0, tiles)
        def _(t):
            c = jnp.where(t >= tiles0, 1, 0)
            start = ((t - c * tiles0) * TILE).astype(jnp.float32)
            at = pl.ds(pl.multiple_of(t * TILE, TILE), TILE)
            p = iota((TILE, F), 0).astype(jnp.float32) + start
            member = (lanes2[c, 0:1, :] <= p) & (p < lanes2[c, 1:2, :])
            member_of = jnp.where(member, 1.0, 0.0).astype(jnp.bfloat16)
            p1 = iota((TILE, SLOTS), 0).astype(jnp.float32) + (start + 1.0)
            hot = dot(member_of, rank2[c]) == p1
            onehot = jnp.where(hot, 1.0, 0.0).astype(jnp.bfloat16)
            oh_all[at, :] = onehot
            seen = dot(onehot, dist2[c])
            seen = jnp.where(member, seen[:, 0:F] + seen[:, F:2 * F], 0.0)
            half = iota((TILE, F), 1) < ATOMS
            d = jnp.sum(jnp.where(half, seen, 0.0), axis=1, keepdims=True)
            e = jnp.sum(jnp.where(half, 0.0, seen), axis=1, keepdims=True)
            centres = iota((TILE, RBF), 1).astype(jnp.float32) * (cutoff / (RBF - 1))
            apart = d - centres
            radial = jnp.exp(-gamma * apart * apart).astype(jnp.bfloat16)
            bias = jnp.concatenate([rb[0:1], rb[1:2]], axis=1)
            hidden = dot(radial, rw_both[...])
            grown = jnp.exp2(hidden * math.log2(math.e) + (bias * math.log2(math.e) - 1.0))
            hidden = jnp.log(grown + 0.5).astype(jnp.bfloat16)
            bias = jnp.concatenate([fb[0:1], fb[1:2]], axis=1)
            kern = ((dot(hidden, fw_both[...]) + bias) * e).astype(jnp.bfloat16)
            kern_all[at, :] = kern[:, F:2 * F]
            for copy in copies(t):
                copy.start()
            rows = pl.ds(pl.multiple_of(c * ATOMS, ATOMS), ATOMS)
            acc[rows, :] += add_pairs(
                onehot, kern[:, 0:F], near2[c], orep2[c], rrep2[c], start
            )

    @pl.when(jnp.logical_not(fits))
    def _():
        slow_cells(
            0, coords, table_ref, vhl, rw, rb, fw, fb,
            scan, slot_s, oh1, near2.at[0], w3, orep, rrep, lanes, acc,
        )

    state = finish(0, coords, state_ref, acc, ow, ob, nw, nb)
    out_ref[...] = state
    next_ref[...] = dense(state, iw[1])

    @pl.loop(0, meta[5])
    def _(t):
        for copy in copies(t):
            copy.wait()


def second_block(
    meta, region, packs, state_ref, table_ref, slots, orep2, rrep2, oh_hbm, kern_hbm,
    rw, rb, fw, fb, ow, ob, nw, nb,
    out_ref,
    vhl, coords, scan, oh1, near2, acc, oh_all, kern_all, slot_s, w3, orep, rrep, lanes,
    osem, ksem,
):
    def copies(t):
        at = pl.ds(pl.multiple_of(t * TILE, TILE), TILE)
        return (
            pltpu.make_async_copy(oh_hbm.at[at], oh_all.at[at], osem.at[t]),
            pltpu.make_async_copy(kern_hbm.at[at], kern_all.at[at], ksem.at[t]),
        )

    tiles = meta[5]

    @pl.loop(0, tiles)
    def _(t):
        for copy in copies(t):
            copy.start()

    place_packs(packs, coords)
    split_values(region, vhl)
    acc[...] = jnp.zeros_like(acc)

    @pl.when(meta[6] == 0)
    def _():
        @pl.loop(0, 2)
        def _(c):
            pick_rows(slots, oh1, c)
            near2[c] = dot(oh1[...], vhl[...]).astype(jnp.bfloat16)

        @pl.loop(0, tiles)
        def _(t):
            for copy in copies(t):
                copy.wait()
            c = jnp.where(t >= meta[4], 1, 0)
            start = ((t - c * meta[4]) * TILE).astype(jnp.float32)
            at = pl.ds(pl.multiple_of(t * TILE, TILE), TILE)
            rows = pl.ds(pl.multiple_of(c * ATOMS, ATOMS), ATOMS)
            acc[rows, :] += add_pairs(
                oh_all[at, :], kern_all[at, :], near2[c], orep2[c], rrep2[c], start
            )

    @pl.when(meta[6] != 0)
    def _():
        fill_scan(scan)
        slow_cells(
            1, coords, table_ref, vhl, rw, rb, fw, fb,
            scan, slot_s, oh1, near2.at[0], w3, orep, rrep, lanes, acc,
        )

    out_ref[...] = finish(1, coords, state_ref, acc, ow, ob, nw, nb)


STATE = jax.ShapeDtypeStruct((2 * ATOMS, F), jnp.float32)
BIG = CAP * TILE
BF = jnp.bfloat16
LOCAL = pltpu.CompilerParams(vmem_limit_bytes=60 << 20)


def run_first(region, packs, state, table, *weights):
    return pl.pallas_call(
        first_block,
        out_shape=(
            STATE,
            STATE,
            jax.ShapeDtypeStruct((16, ROWS), jnp.float32),
            jax.ShapeDtypeStruct((2, ATOMS, F), jnp.float32),
            jax.ShapeDtypeStruct((2, ATOMS, F), jnp.float32),
            jax.ShapeDtypeStruct((8,), jnp.int32),
            jax.ShapeDtypeStruct((BIG, SLOTS), BF),
            jax.ShapeDtypeStruct((BIG, F), BF),
        ),
        in_specs=[VMEM] * 13,
        out_specs=(VMEM, VMEM, VMEM, VMEM, VMEM, SMEM, ANY, ANY),
        scratch_shapes=[
            pltpu.VMEM((ROWS, 2 * F), BF),
            pltpu.VMEM((8, ROWS), jnp.float32),
            pltpu.VMEM((F, 2 * F), BF),
            pltpu.VMEM((SLOTS, ROWS), BF),
            pltpu.VMEM((2, SLOTS, 2 * F), BF),
            pltpu.VMEM((2, F, SLOTS), BF),
            pltpu.VMEM((2, SLOTS, 2 * F), BF),
            pltpu.VMEM((2, 8, F), jnp.float32),
            pltpu.VMEM((2 * ATOMS, F), jnp.float32),
            pltpu.VMEM((BIG, SLOTS), BF),
            pltpu.VMEM((BIG, F), BF),
            pltpu.VMEM((RBF, 2 * F), BF),
            pltpu.VMEM((2 * F, 2 * F), BF),
            pltpu.VMEM((8, ROWS), jnp.float32),
            pltpu.VMEM((256, 3 * SLOTS), BF),
            pltpu.VMEM((ATOMS, F), jnp.float32),
            pltpu.VMEM((ATOMS, F), jnp.float32),
            pltpu.VMEM((8, 2 * F), jnp.float32),
            pltpu.SemaphoreType.DMA((CAP,)),
            pltpu.SemaphoreType.DMA((CAP,)),
        ],
        compiler_params=LOCAL,
    )(region, packs, state, table, *weights)


def run_second(meta, region, packs, state, table, slots, orep, rrep, oh, kern, *weights):
    return pl.pallas_call(
        second_block,
        out_shape=STATE,
        in_specs=[SMEM] + [VMEM] * 7 + [ANY, ANY] + [VMEM] * 8,
        out_specs=VMEM,
        scratch_shapes=[
            pltpu.VMEM((ROWS, 2 * F), BF),
            pltpu.VMEM((8, ROWS), jnp.float32),
            pltpu.VMEM((F, 2 * F), BF),
            pltpu.VMEM((SLOTS, ROWS), BF),
            pltpu.VMEM((2, SLOTS, 2 * F), BF),
            pltpu.VMEM((2 * ATOMS, F), jnp.float32),
            pltpu.VMEM((BIG, SLOTS), BF),
            pltpu.VMEM((BIG, F), BF),
            pltpu.VMEM((8, ROWS), jnp.float32),
            pltpu.VMEM((256, 3 * SLOTS), BF),
            pltpu.VMEM((ATOMS, F), jnp.float32),
            pltpu.VMEM((ATOMS, F), jnp.float32),
            pltpu.VMEM((8, 2 * F), jnp.float32),
            pltpu.SemaphoreType.DMA((CAP,)),
            pltpu.SemaphoreType.DMA((CAP,)),
        ],
        compiler_params=LOCAL,
    )(meta, region, packs, state, table, slots, orep, rrep, oh, kern, *weights)


def shards(
    features,
    positions,
    counts,
    rbf_weight,
    rbf_bias,
    filter_weight,
    filter_bias,
    input_weight,
    output_weight,
    output_bias,
    final_weight,
    final_bias,
):
    state = features.reshape(2 * ATOMS, F)
    table = jnp.asarray(region_table())
    filters = (rbf_weight, rbf_bias, filter_weight, filter_bias)
    atomwise = (output_weight, output_bias, final_weight, final_bias)
    region, packs = start_halo(
        counts.reshape(2), state, positions.reshape(2, 3, ATOMS), input_weight
    )
    state, values, slots, orep, rrep, meta, oh, kern = run_first(
        region, packs, state, table, *filters, *atomwise, input_weight
    )
    region = later_halo(values)
    state = run_second(
        meta, region, packs, state, table, slots, orep, rrep, oh, kern, *filters, *atomwise
    )
    return state.reshape(features.shape)


def solution(mesh):
    cells = P("gx", "gy", "gz", None, None)
    placed = (cells, cells, P("gx", "gy", "gz")) + (P(),) * 9
    return jax.shard_map(
        shards, mesh=mesh, in_specs=placed, out_specs=cells, check_vma=False
    )
```

```python
import math

import jax
import jax.numpy as jnp
import numpy as np
from jax import lax
from jax.experimental import pallas as pl
from jax.experimental.pallas import tpu as pltpu
from jax.sharding import PartitionSpec as P

F = 128
RBF = 64
ATOMS = 64
BLOCKS = 2

cell_edge = 8.0
cutoff = 5.0
gamma = 10.0
scale_sum = 0.125

ROWS = 36 * ATOMS
PACKS = ROWS // F
SLOTS = 512
TILE = 512
CAP = 24
HI = lax.Precision.HIGHEST
VMEM = pl.BlockSpec(memory_space=pltpu.VMEM)
ANY = pl.BlockSpec(memory_space=pl.ANY)
SMEM = pl.BlockSpec(memory_space=pltpu.SMEM)


def softplus(v):
    return jnp.maximum(v, 0.0) + jnp.log(1.0 + jnp.exp(-jnp.abs(v))) - math.log(2.0)


def region_table():
    table = np.zeros((8, ROWS), np.float32)
    for dx in range(3):
        for dy in range(3):
            for k, z in enumerate((0, 1, 2, -1)):
                q = (dx * 3 + dy) * 4 + k
                at = slice(q * ATOMS, (q + 1) * ATOMS)
                table[0, at] = cell_edge * (dx - 1)
                table[1, at] = cell_edge * (dy - 1)
                table[2, at] = cell_edge * z
                table[3, at] = np.arange(ATOMS) + 1 if q == 16 else 100
                table[4, at] = np.arange(ATOMS) + 1 if q == 17 else 100
    return table


def iota(shape, dim):
    return lax.broadcasted_iota(jnp.int32, shape, dim)


def dot(a, b):
    return jnp.dot(a, b, preferred_element_type=jnp.float32)


def pieces3(x):
    a = x.astype(jnp.bfloat16)
    r = x - a.astype(jnp.float32)
    b = r.astype(jnp.bfloat16)
    c = (r - b.astype(jnp.float32)).astype(jnp.bfloat16)
    return a, b, c


def slow_cells(
    b, coords, table_ref, vhl, rw_ref, rb_ref, fw_ref, fb_ref,
    scan_ref, slot_of, oh1, near, w3, orep, rrep, lanes, acc,
):
    acc[...] = jnp.zeros_like(acc)

    @pl.loop(0, 2)
    def _(c):
        base = c * ATOMS
        pick = iota((ATOMS, F), 1) == iota((ATOMS, F), 0) + base
        own = coords[:, 8 * F:9 * F]

        def column(r):
            return jnp.sum(jnp.where(pick, own[r:r + 1, :], 0.0), axis=1, keepdims=True)

        ox, oy, oz, olive = column(0), column(1), column(2), column(3)
        zshift = cell_edge * c.astype(jnp.float32)

        def placed(at):
            px = coords[0:1, at] + table_ref[0:1, at]
            py = coords[1:2, at] + table_ref[1:2, at]
            pz = coords[2:3, at] + (table_ref[2:3, at] - zshift)
            return px, py, pz

        anys = []
        for k in range(PACKS):
            at = slice(k * F, (k + 1) * F)
            px, py, pz = placed(at)
            dx, dy, dz = px - ox, py - oy, pz - oz
            near_enough = jnp.where(dx * dx + dy * dy + dz * dz < cutoff * cutoff, olive, 0.0)
            hit = jnp.max(near_enough, axis=0, keepdims=True) * coords[3:4, at]
            anys.append(jnp.broadcast_to(hit, (8, F)))
        stacked = jnp.concatenate(anys, axis=0)
        scanned = dot(stacked.astype(jnp.bfloat16), scan_ref[...])
        carry = jnp.zeros((8, F), jnp.float32)
        for k in range(PACKS):
            part = scanned[k * 8:(k + 1) * 8]
            slot_of[:, k * F:(k + 1) * F] = jnp.where(
                anys[k] > 0.5, carry + part[:, 0:F] - 1.0, -1.0
            )
            carry = carry + part[:, F:2 * F]
        found = jnp.max(carry).astype(jnp.int32)

        @pl.loop(0, (found + SLOTS - 1) // SLOTS)
        def _(h):
            first = h * SLOTS
            want = (iota((SLOTS, F), 0) + first).astype(jnp.float32)
            for k in range(PACKS):
                at = slice(k * F, (k + 1) * F)
                oh1[:, at] = jnp.where(slot_of[0:1, at] == want, 1.0, 0.0).astype(jnp.bfloat16)
            near[...] = dot(oh1[...], vhl[...]).astype(jnp.bfloat16)
            px, py, pz = placed(slice(0, ROWS))
            ids = table_ref[pl.ds(3 + c, 1), :].astype(jnp.bfloat16)
            rows = [*pieces3(px), *pieces3(py), *pieces3(pz), ids]
            rows = jnp.concatenate(
                [r.astype(jnp.float32) for r in rows] + [jnp.zeros((6, ROWS), jnp.float32)], axis=0
            ).astype(jnp.bfloat16)
            packed = lax.dot_general(
                rows, oh1[...], (((1,), (1,)), ((), ())), preferred_element_type=jnp.float32
            )
            cx = packed[0:1] + packed[1:2] + packed[2:3]
            cy = packed[3:4] + packed[4:5] + packed[5:6]
            cz = packed[6:7] + packed[7:8] + packed[8:9]
            cid = packed[9:10]
            dx, dy, dz = cx - ox, cy - oy, cz - oz
            dist = jnp.sqrt(dx * dx + dy * dy + dz * dz)
            me = (iota((ATOMS, SLOTS), 0) + 1).astype(jnp.float32)
            keep = (dist < cutoff) & (cid > 0.5) & (cid != me) & (olive > 0.5)
            ones = jnp.where(keep, 1.0, 0.0)
            envelope = jnp.where(
                keep, 0.5 * (jnp.cos(math.pi * dist / cutoff) + 1.0), 0.0
            )
            dist = jnp.where(keep, dist, 0.0)
            parts = jnp.concatenate(
                [ones[:, k * F:(k + 1) * F] for k in range(SLOTS // F)], axis=0
            ).astype(jnp.bfloat16)
            scanned = dot(parts, scan_ref[...])
            run = jnp.zeros((ATOMS, F), jnp.float32)
            ranks = []
            for k in range(SLOTS // F):
                part = scanned[k * ATOMS:(k + 1) * ATOMS]
                ranks.append(run + part[:, 0:F])
                run = run + part[:, F:2 * F]
            strict = jnp.where(
                iota((ATOMS, ATOMS), 0) > iota((ATOMS, ATOMS), 1), 1.0, 0.0
            )
            offset = jnp.dot(strict, run, precision=HI, preferred_element_type=jnp.float32)
            orep[...] = offset
            rrep[...] = run
            pairs = jnp.max(offset + run).astype(jnp.int32)
            offset_all = jnp.concatenate([offset] * (SLOTS // F), axis=1)
            index = jnp.where(keep, offset_all + jnp.concatenate(ranks, axis=1), 0.0).astype(
                jnp.int32
            )
            w3[0:64, 0:SLOTS] = (index & ~16383).astype(jnp.float32).astype(jnp.bfloat16)
            w3[64:128, 0:SLOTS] = (index & (127 * 128)).astype(jnp.float32).astype(jnp.bfloat16)
            w3[128:192, 0:SLOTS] = (index & 127).astype(jnp.float32).astype(jnp.bfloat16)
            for n, parts3 in enumerate((pieces3(dist), pieces3(envelope))):
                for r, piece in enumerate(parts3):
                    w3[r * 64:(r + 1) * 64, (n + 1) * SLOTS:(n + 2) * SLOTS] = piece
            w3[192:256, :] = jnp.zeros((64, 3 * SLOTS), jnp.bfloat16)
            spread = ((iota((ATOMS, 2 * F), 1) & 63) == iota((ATOMS, 2 * F), 0)) & (
                iota((ATOMS, 2 * F), 1) < 192
            )
            two = jnp.concatenate([offset, offset], axis=1)
            low = jnp.sum(jnp.where(spread, two, 0.0), axis=0, keepdims=True)
            two = jnp.concatenate([run, run], axis=1)
            count = jnp.sum(jnp.where(spread, two, 0.0), axis=0, keepdims=True)
            lanes[0:1, :] = low
            lanes[1:2, :] = low + count

            @pl.loop(0, (pairs + TILE - 1) // TILE)
            def _(t):
                start = (t * TILE).astype(jnp.float32)
                p = iota((TILE, 2 * F), 0).astype(jnp.float32) + start
                member = jnp.where((lanes[0:1, :] <= p) & (p < lanes[1:2, :]), 1.0, 0.0)
                member = member.astype(jnp.bfloat16)
                p1 = iota((TILE, SLOTS), 0).astype(jnp.float32) + (start + 1.0)
                hot = dot(member, w3[:, 0:SLOTS]) == p1
                d = jnp.sum(
                    jnp.where(hot, dot(member, w3[:, SLOTS:2 * SLOTS]), 0.0), axis=1, keepdims=True
                )
                e = jnp.sum(
                    jnp.where(hot, dot(member, w3[:, 2 * SLOTS:3 * SLOTS]), 0.0),
                    axis=1,
                    keepdims=True,
                )
                onehot = jnp.where(hot, 1.0, 0.0).astype(jnp.bfloat16)
                got = dot(onehot, near[...])
                got = got[:, 0:F] + got[:, F:2 * F]
                centres = iota((TILE, RBF), 1).astype(jnp.float32) * (cutoff / (RBF - 1))
                apart = d - centres
                radial = jnp.exp(-gamma * apart * apart).astype(jnp.bfloat16)
                hidden = softplus(dot(radial, rw_ref[b]) + rb_ref[b:b + 1]).astype(jnp.bfloat16)
                kern = ((dot(hidden, fw_ref[b]) + fb_ref[b:b + 1]) * e).astype(jnp.bfloat16)
                prod = kern.astype(jnp.float32) * got
                top = prod.astype(jnp.bfloat16)
                rest = (prod - top.astype(jnp.float32)).astype(jnp.bfloat16)
                pl_ = iota((ATOMS, TILE), 1).astype(jnp.float32) + start
                lo = jnp.concatenate([orep[...]] * (TILE // F), axis=1)
                hi = lo + jnp.concatenate([rrep[...]] * (TILE // F), axis=1)
                back = jnp.where((lo <= pl_) & (pl_ < hi), 1.0, 0.0).astype(jnp.bfloat16)
                summed = dot(back, jnp.concatenate([top, rest], axis=1))
                at = pl.ds(pl.multiple_of(base, ATOMS), ATOMS)
                acc[at, :] += summed[:, 0:F] + summed[:, F:2 * F]


def dense(x, w):
    return jnp.dot(x, w, precision=HI, preferred_element_type=jnp.float32)


def region_rows(dx, dy, k, cells):
    return pl.ds((((dx + 1) * 3 + dy + 1) * 4 + k) * ATOMS, cells * ATOMS)


def neighbours():
    return [
        (ox, oy, oz)
        for ox in (-1, 0, 1)
        for oy in (-1, 0, 1)
        for oz in (-1, 0, 1)
        if (ox, oy, oz) != (0, 0, 0)
    ]


def device_at(offset):
    return tuple(
        lax.rem(lax.axis_index(a) + (o + lax.axis_size(a)), lax.axis_size(a))
        for a, o in zip(("gx", "gy", "gz"), offset)
    )


def greet(offsets):
    barrier = pltpu.get_barrier_semaphore()
    for o in offsets:
        pl.semaphore_signal(
            barrier, inc=1, device_id=device_at(o), device_id_type=pl.DeviceIdType.MESH
        )
    pl.semaphore_wait(barrier, len(offsets))


FACES = [(0, 1, 0), (0, -1, 0), (0, 0, 1), (0, 0, -1), (1, 0, 0), (-1, 0, 0)]


def spread_values(vals, region, ssem, rsem):
    copies = {}

    def send(name, src, dst, to):
        n = len(copies)
        copies[name] = pltpu.make_async_remote_copy(
            src_ref=src,
            dst_ref=region.at[dst],
            send_sem=ssem.at[n],
            recv_sem=rsem.at[n],
            device_id=device_at(to),
            device_id_type=pl.DeviceIdType.MESH,
        )
        copies[name].start()

    def cells(dy, k, n):
        if dy == 0 and k < 2:
            return vals.at[pl.ds(k * ATOMS, n * ATOMS)]
        return region.at[region_rows(0, dy, k, n)]

    def send_z(dy):
        send(("z", dy, 3), cells(dy, 1, 1), region_rows(0, dy, 3, 1), (0, 0, 1))
        send(("z", dy, 2), cells(dy, 0, 1), region_rows(0, dy, 2, 1), (0, 0, -1))

    def send_x(dy, k):
        send(("x", dy, k, 1), cells(dy, k, 2), region_rows(-1, dy, k, 2), (1, 0, 0))
        send(("x", dy, k, -1), cells(dy, k, 2), region_rows(1, dy, k, 2), (-1, 0, 0))

    send(("y", -1), cells(0, 0, 2), region_rows(0, -1, 0, 2), (0, 1, 0))
    send(("y", 1), cells(0, 0, 2), region_rows(0, 1, 0, 2), (0, -1, 0))
    send_z(0)
    send_x(0, 0)
    region[region_rows(0, 0, 0, 2), :] = vals[...]
    for k in (2, 3):
        copies["z", 0, k].wait_recv()
    send_x(0, 2)
    for dy in (-1, 1):
        copies["y", dy].wait_recv()
        send_z(dy)
        send_x(dy, 0)
    for dy in (-1, 1):
        for k in (2, 3):
            copies["z", dy, k].wait_recv()
        send_x(dy, 2)
    for name, copy in copies.items():
        if name[0] == "x":
            copy.wait_recv()
    for copy in copies.values():
        copy.wait_send()


def first_comm(
    counts_ref, state_ref, pos_ref, iw_ref, region, packs, vals, pack, ssem, rsem, psend, precv
):
    live = [
        jnp.where(iota((1, ATOMS), 1) < counts_ref[c], 1.0, 0.0) for c in range(2)
    ]
    rows = [
        jnp.concatenate([pos_ref[c], live[c], jnp.zeros((4, ATOMS), jnp.float32)], axis=0)
        for c in range(2)
    ]
    pack[...] = jnp.concatenate(rows, axis=1)
    vals[...] = dense(state_ref[...], iw_ref[0])
    greet(neighbours())
    copies = []
    for n, (ox, oy, oz) in enumerate(neighbours()):
        slot = (1 - ox) * 9 + (1 - oy) * 3 + (1 - oz)
        copies.append(
            pltpu.make_async_remote_copy(
                src_ref=pack,
                dst_ref=packs.at[slot],
                send_sem=psend.at[n],
                recv_sem=precv.at[n],
                device_id=device_at((ox, oy, oz)),
                device_id_type=pl.DeviceIdType.MESH,
            )
        )
        copies[-1].start()
    packs[13] = pack[...]
    spread_values(vals, region, ssem, rsem)
    for copy in copies:
        copy.wait_recv()
    for copy in copies:
        copy.wait_send()


def later_comm(vals_ref, region, ssem, rsem):
    greet(FACES)
    spread_values(vals_ref, region, ssem, rsem)


REGION = jax.ShapeDtypeStruct((ROWS, F), jnp.float32)
PACKED = jax.ShapeDtypeStruct((27, 8, F), jnp.float32)


def start_halo(counts, state, positions, input_weight):
    return pl.pallas_call(
        first_comm,
        out_shape=(REGION, PACKED),
        in_specs=[SMEM, VMEM, VMEM, VMEM],
        out_specs=(VMEM, VMEM),
        scratch_shapes=[
            pltpu.VMEM((2 * ATOMS, F), jnp.float32),
            pltpu.VMEM((8, F), jnp.float32),
            pltpu.SemaphoreType.DMA((20,)),
            pltpu.SemaphoreType.DMA((20,)),
            pltpu.SemaphoreType.DMA((26,)),
            pltpu.SemaphoreType.DMA((26,)),
        ],
        compiler_params=pltpu.CompilerParams(collective_id=0, has_side_effects=True),
    )(counts, state, positions, input_weight)


def later_halo(vals):
    return pl.pallas_call(
        later_comm,
        out_shape=REGION,
        in_specs=[VMEM],
        out_specs=VMEM,
        scratch_shapes=[pltpu.SemaphoreType.DMA((20,)), pltpu.SemaphoreType.DMA((20,))],
        compiler_params=pltpu.CompilerParams(collective_id=1, has_side_effects=True),
    )(vals)


def split_values(region, vhl):
    @pl.loop(0, ROWS // 256)
    def _(k):
        at = pl.ds(pl.multiple_of(k * 256, 256), 256)
        v = region[at, :]
        top = v.astype(jnp.bfloat16)
        vhl[at, 0:F] = top
        vhl[at, F:2 * F] = (v - top.astype(jnp.float32)).astype(jnp.bfloat16)


def place_packs(packs, coords):
    lower = iota((8, F), 1) < ATOMS
    for q in range(9):
        coords[:, 2 * q * F:(2 * q + 1) * F] = packs[3 * q + 1]
        coords[:, (2 * q + 1) * F:(2 * q + 2) * F] = jnp.where(
            lower, packs[3 * q + 2], packs[3 * q]
        )


def fill_scan(scan):
    upper = iota((F, F), 0) <= iota((F, F), 1)
    scan[:, 0:F] = jnp.where(upper, 1.0, 0.0).astype(jnp.bfloat16)
    scan[:, F:2 * F] = jnp.ones((F, F), jnp.bfloat16)


def pick_rows(slots, oh1, c):
    want = iota((SLOTS, F), 0).astype(jnp.float32)
    for k in range(PACKS):
        at = slice(k * F, (k + 1) * F)
        row = slots[pl.ds(8 * c, 1), at]
        oh1[:, at] = jnp.where(row == want, 1.0, 0.0).astype(jnp.bfloat16)


def finish(b, coords, state_ref, acc, ow, ob, nw, nb):
    mixed = softplus(dense(acc[...] * scale_sum, ow[b]) + ob[b:b + 1])
    update = dense(mixed, nw[b]) + nb[b:b + 1]
    diag = iota((F, F), 0) == iota((F, F), 1)
    live = jnp.sum(jnp.where(diag, coords[3:4, 8 * F:9 * F], 0.0), axis=1, keepdims=True)
    return (state_ref[...] + update) * live


def add_pairs(onehot, kern, near, low, size, start):
    got = dot(onehot, near)
    got = got[:, 0:F] + got[:, F:2 * F]
    prod = kern.astype(jnp.float32) * got
    top = prod.astype(jnp.bfloat16)
    rest = (prod - top.astype(jnp.float32)).astype(jnp.bfloat16)
    p = iota((ATOMS, TILE), 1).astype(jnp.float32) + start
    lo = jnp.concatenate([low] * (TILE // F), axis=1)
    hi = lo + jnp.concatenate([size] * (TILE // F), axis=1)
    back = jnp.where((lo <= p) & (p < hi), 1.0, 0.0).astype(jnp.bfloat16)
    summed = dot(back, jnp.concatenate([top, rest], axis=1))
    return summed[:, 0:F] + summed[:, F:2 * F]


def first_block(
    region, packs, state_ref, table_ref,
    rw, rb, fw, fb, ow, ob, nw, nb, iw,
    out_ref, next_ref, slots, orep2, rrep2, meta, oh_hbm, kern_hbm,
    vhl, coords, scan, oh1, near2, rank2, dist2, lanes2, acc, oh_all, kern_all,
    rw_both, fw_both, slot_s, w3, orep, rrep, lanes, osem, ksem,
):
    place_packs(packs, coords)
    split_values(region, vhl)
    fill_scan(scan)
    rw_both[:, 0:F] = rw[0]
    rw_both[:, F:2 * F] = rw[1]
    fw_both[...] = jnp.zeros_like(fw_both)
    fw_both[0:F, 0:F] = fw[0]
    fw_both[F:2 * F, F:2 * F] = fw[1]
    acc[...] = jnp.zeros_like(acc)

    @pl.loop(0, 2)
    def _(c):
        base = c * ATOMS
        pick = iota((ATOMS, F), 1) == iota((ATOMS, F), 0) + base
        own = coords[:, 8 * F:9 * F]

        def column(r):
            return jnp.sum(jnp.where(pick, own[r:r + 1, :], 0.0), axis=1, keepdims=True)

        ox, oy, oz, olive = column(0), column(1), column(2), column(3)
        zshift = cell_edge * c.astype(jnp.float32)

        def placed(at):
            px = coords[0:1, at] + table_ref[0:1, at]
            py = coords[1:2, at] + table_ref[1:2, at]
            pz = coords[2:3, at] + (table_ref[2:3, at] - zshift)
            return px, py, pz

        anys = []
        for k in range(PACKS):
            at = slice(k * F, (k + 1) * F)
            px, py, pz = placed(at)
            dx, dy, dz = px - ox, py - oy, pz - oz
            near_enough = jnp.where(dx * dx + dy * dy + dz * dz < cutoff * cutoff, olive, 0.0)
            hit = jnp.max(near_enough, axis=0, keepdims=True) * coords[3:4, at]
            anys.append(jnp.broadcast_to(hit, (8, F)))
        scanned = dot(jnp.concatenate(anys, axis=0).astype(jnp.bfloat16), scan[...])
        carry = jnp.zeros((8, F), jnp.float32)
        mine = pl.ds(pl.multiple_of(8 * c, 8), 8)
        for k in range(PACKS):
            part = scanned[k * 8:(k + 1) * 8]
            slots[mine, k * F:(k + 1) * F] = jnp.where(
                anys[k] > 0.5, carry + part[:, 0:F] - 1.0, -1.0
            )
            carry = carry + part[:, F:2 * F]
        meta[c] = jnp.max(carry).astype(jnp.int32)

        pick_rows(slots, oh1, c)
        near2[c] = dot(oh1[...], vhl[...]).astype(jnp.bfloat16)
        px, py, pz = placed(slice(0, ROWS))
        ids = table_ref[pl.ds(3 + c, 1), :].astype(jnp.bfloat16)
        rows = [*pieces3(px), *pieces3(py), *pieces3(pz), ids]
        rows = jnp.concatenate(
            [r.astype(jnp.float32) for r in rows] + [jnp.zeros((6, ROWS), jnp.float32)], axis=0
        ).astype(jnp.bfloat16)
        packed = lax.dot_general(
            rows, oh1[...], (((1,), (1,)), ((), ())), preferred_element_type=jnp.float32
        )
        cx = packed[0:1] + packed[1:2] + packed[2:3]
        cy = packed[3:4] + packed[4:5] + packed[5:6]
        cz = packed[6:7] + packed[7:8] + packed[8:9]
        cid = packed[9:10]
        dx, dy, dz = cx - ox, cy - oy, cz - oz
        dist = jnp.sqrt(dx * dx + dy * dy + dz * dz)
        me = (iota((ATOMS, SLOTS), 0) + 1).astype(jnp.float32)
        keep = (dist < cutoff) & (cid > 0.5) & (cid != me) & (olive > 0.5)
        ones = jnp.where(keep, 1.0, 0.0)
        envelope = jnp.where(keep, 0.5 * (jnp.cos(math.pi * dist / cutoff) + 1.0), 0.0)
        both = jnp.concatenate([jnp.where(keep, dist, 0.0), envelope], axis=0)
        for k in range(SLOTS // F):
            at = slice(k * F, (k + 1) * F)
            turned = both[:, at].T
            top = turned.astype(jnp.bfloat16)
            dist2[c, at, 0:F] = top
            dist2[c, at, F:2 * F] = (turned - top.astype(jnp.float32)).astype(jnp.bfloat16)
        parts = jnp.concatenate(
            [ones[:, k * F:(k + 1) * F] for k in range(SLOTS // F)], axis=0
        ).astype(jnp.bfloat16)
        scanned = dot(parts, scan[...])
        run = jnp.zeros((ATOMS, F), jnp.float32)
        ranks = []
        for k in range(SLOTS // F):
            part = scanned[k * ATOMS:(k + 1) * ATOMS]
            ranks.append(run + part[:, 0:F])
            run = run + part[:, F:2 * F]
        strict = jnp.where(iota((ATOMS, ATOMS), 0) > iota((ATOMS, ATOMS), 1), 1.0, 0.0)
        offset = jnp.dot(strict, run, precision=HI, preferred_element_type=jnp.float32)
        orep2[c] = offset
        rrep2[c] = run
        meta[2 + c] = jnp.max(offset + run).astype(jnp.int32)
        offset_all = jnp.concatenate([offset] * (SLOTS // F), axis=1)
        index = jnp.where(keep, offset_all + jnp.concatenate(ranks, axis=1), 0.0).astype(jnp.int32)
        rank2[c, 0:64, :] = (index & ~255).astype(jnp.float32).astype(jnp.bfloat16)
        rank2[c, 64:128, :] = (index & 255).astype(jnp.float32).astype(jnp.bfloat16)
        spread = (iota((ATOMS, F), 1) & 63) == iota((ATOMS, F), 0)
        low = jnp.sum(jnp.where(spread, offset, 0.0), axis=0, keepdims=True)
        count = jnp.sum(jnp.where(spread, run, 0.0), axis=0, keepdims=True)
        lanes2[c, 0:1, :] = low
        lanes2[c, 1:2, :] = low + count

    tiles0 = (meta[2] + TILE - 1) // TILE
    tiles = tiles0 + (meta[3] + TILE - 1) // TILE
    fits = (meta[0] <= SLOTS) & (meta[1] <= SLOTS) & (tiles <= CAP)
    meta[4] = tiles0
    meta[5] = jnp.where(fits, tiles, 0)
    meta[6] = jnp.where(fits, 0, 1)
    meta[7] = 0

    def copies(t):
        at = pl.ds(pl.multiple_of(t * TILE, TILE), TILE)
        return (
            pltpu.make_async_copy(oh_all.at[at], oh_hbm.at[at], osem.at[t]),
            pltpu.make_async_copy(kern_all.at[at], kern_hbm.at[at], ksem.at[t]),
        )

    @pl.when(fits)
    def _():
        @pl.loop(0, tiles)
        def _(t):
            c = jnp.where(t >= tiles0, 1, 0)
            start = ((t - c * tiles0) * TILE).astype(jnp.float32)
            at = pl.ds(pl.multiple_of(t * TILE, TILE), TILE)
            p = iota((TILE, F), 0).astype(jnp.float32) + start
            member = (lanes2[c, 0:1, :] <= p) & (p < lanes2[c, 1:2, :])
            member_of = jnp.where(member, 1.0, 0.0).astype(jnp.bfloat16)
            p1 = iota((TILE, SLOTS), 0).astype(jnp.float32) + (start + 1.0)
            hot = dot(member_of, rank2[c]) == p1
            onehot = jnp.where(hot, 1.0, 0.0).astype(jnp.bfloat16)
            oh_all[at, :] = onehot
            seen = dot(onehot, dist2[c])
            seen = jnp.where(member, seen[:, 0:F] + seen[:, F:2 * F], 0.0)
            half = iota((TILE, F), 1) < ATOMS
            d = jnp.sum(jnp.where(half, seen, 0.0), axis=1, keepdims=True)
            e = jnp.sum(jnp.where(half, 0.0, seen), axis=1, keepdims=True)
            centres = iota((TILE, RBF), 1).astype(jnp.float32) * (cutoff / (RBF - 1))
            apart = d - centres
            radial = jnp.exp(-gamma * apart * apart).astype(jnp.bfloat16)
            bias = jnp.concatenate([rb[0:1], rb[1:2]], axis=1)
            hidden = dot(radial, rw_both[...])
            grown = jnp.exp2(hidden * math.log2(math.e) + (bias * math.log2(math.e) - 1.0))
            hidden = jnp.log(grown + 0.5).astype(jnp.bfloat16)
            bias = jnp.concatenate([fb[0:1], fb[1:2]], axis=1)
            kern = ((dot(hidden, fw_both[...]) + bias) * e).astype(jnp.bfloat16)
            kern_all[at, :] = kern[:, F:2 * F]
            for copy in copies(t):
                copy.start()
            rows = pl.ds(pl.multiple_of(c * ATOMS, ATOMS), ATOMS)
            acc[rows, :] += add_pairs(
                onehot, kern[:, 0:F], near2[c], orep2[c], rrep2[c], start
            )

    @pl.when(jnp.logical_not(fits))
    def _():
        slow_cells(
            0, coords, table_ref, vhl, rw, rb, fw, fb,
            scan, slot_s, oh1, near2.at[0], w3, orep, rrep, lanes, acc,
        )

    state = finish(0, coords, state_ref, acc, ow, ob, nw, nb)
    out_ref[...] = state
    next_ref[...] = dense(state, iw[1])

    @pl.loop(0, meta[5])
    def _(t):
        for copy in copies(t):
            copy.wait()


def second_block(
    meta, region, packs, state_ref, table_ref, slots, orep2, rrep2, oh_hbm, kern_hbm,
    rw, rb, fw, fb, ow, ob, nw, nb,
    out_ref,
    vhl, coords, scan, oh1, near2, acc, oh_all, kern_all, slot_s, w3, orep, rrep, lanes,
    osem, ksem,
):
    def copies(t):
        at = pl.ds(pl.multiple_of(t * TILE, TILE), TILE)
        return (
            pltpu.make_async_copy(oh_hbm.at[at], oh_all.at[at], osem.at[t]),
            pltpu.make_async_copy(kern_hbm.at[at], kern_all.at[at], ksem.at[t]),
        )

    tiles = meta[5]

    @pl.loop(0, tiles)
    def _(t):
        for copy in copies(t):
            copy.start()

    place_packs(packs, coords)
    split_values(region, vhl)
    acc[...] = jnp.zeros_like(acc)

    @pl.when(meta[6] == 0)
    def _():
        @pl.loop(0, 2)
        def _(c):
            pick_rows(slots, oh1, c)
            near2[c] = dot(oh1[...], vhl[...]).astype(jnp.bfloat16)

        @pl.loop(0, tiles)
        def _(t):
            for copy in copies(t):
                copy.wait()
            c = jnp.where(t >= meta[4], 1, 0)
            start = ((t - c * meta[4]) * TILE).astype(jnp.float32)
            at = pl.ds(pl.multiple_of(t * TILE, TILE), TILE)
            rows = pl.ds(pl.multiple_of(c * ATOMS, ATOMS), ATOMS)
            acc[rows, :] += add_pairs(
                oh_all[at, :], kern_all[at, :], near2[c], orep2[c], rrep2[c], start
            )

    @pl.when(meta[6] != 0)
    def _():
        fill_scan(scan)
        slow_cells(
            1, coords, table_ref, vhl, rw, rb, fw, fb,
            scan, slot_s, oh1, near2.at[0], w3, orep, rrep, lanes, acc,
        )

    out_ref[...] = finish(1, coords, state_ref, acc, ow, ob, nw, nb)


STATE = jax.ShapeDtypeStruct((2 * ATOMS, F), jnp.float32)
BIG = CAP * TILE
BF = jnp.bfloat16
LOCAL = pltpu.CompilerParams(vmem_limit_bytes=60 << 20)


def run_first(region, packs, state, table, *weights):
    return pl.pallas_call(
        first_block,
        out_shape=(
            STATE,
            STATE,
            jax.ShapeDtypeStruct((16, ROWS), jnp.float32),
            jax.ShapeDtypeStruct((2, ATOMS, F), jnp.float32),
            jax.ShapeDtypeStruct((2, ATOMS, F), jnp.float32),
            jax.ShapeDtypeStruct((8,), jnp.int32),
            jax.ShapeDtypeStruct((BIG, SLOTS), BF),
            jax.ShapeDtypeStruct((BIG, F), BF),
        ),
        in_specs=[VMEM] * 13,
        out_specs=(VMEM, VMEM, VMEM, VMEM, VMEM, SMEM, ANY, ANY),
        scratch_shapes=[
            pltpu.VMEM((ROWS, 2 * F), BF),
            pltpu.VMEM((8, ROWS), jnp.float32),
            pltpu.VMEM((F, 2 * F), BF),
            pltpu.VMEM((SLOTS, ROWS), BF),
            pltpu.VMEM((2, SLOTS, 2 * F), BF),
            pltpu.VMEM((2, F, SLOTS), BF),
            pltpu.VMEM((2, SLOTS, 2 * F), BF),
            pltpu.VMEM((2, 8, F), jnp.float32),
            pltpu.VMEM((2 * ATOMS, F), jnp.float32),
            pltpu.VMEM((BIG, SLOTS), BF),
            pltpu.VMEM((BIG, F), BF),
            pltpu.VMEM((RBF, 2 * F), BF),
            pltpu.VMEM((2 * F, 2 * F), BF),
            pltpu.VMEM((8, ROWS), jnp.float32),
            pltpu.VMEM((256, 3 * SLOTS), BF),
            pltpu.VMEM((ATOMS, F), jnp.float32),
            pltpu.VMEM((ATOMS, F), jnp.float32),
            pltpu.VMEM((8, 2 * F), jnp.float32),
            pltpu.SemaphoreType.DMA((CAP,)),
            pltpu.SemaphoreType.DMA((CAP,)),
        ],
        compiler_params=LOCAL,
    )(region, packs, state, table, *weights)


def run_second(meta, region, packs, state, table, slots, orep, rrep, oh, kern, *weights):
    return pl.pallas_call(
        second_block,
        out_shape=STATE,
        in_specs=[SMEM] + [VMEM] * 7 + [ANY, ANY] + [VMEM] * 8,
        out_specs=VMEM,
        scratch_shapes=[
            pltpu.VMEM((ROWS, 2 * F), BF),
            pltpu.VMEM((8, ROWS), jnp.float32),
            pltpu.VMEM((F, 2 * F), BF),
            pltpu.VMEM((SLOTS, ROWS), BF),
            pltpu.VMEM((2, SLOTS, 2 * F), BF),
            pltpu.VMEM((2 * ATOMS, F), jnp.float32),
            pltpu.VMEM((BIG, SLOTS), BF),
            pltpu.VMEM((BIG, F), BF),
            pltpu.VMEM((8, ROWS), jnp.float32),
            pltpu.VMEM((256, 3 * SLOTS), BF),
            pltpu.VMEM((ATOMS, F), jnp.float32),
            pltpu.VMEM((ATOMS, F), jnp.float32),
            pltpu.VMEM((8, 2 * F), jnp.float32),
            pltpu.SemaphoreType.DMA((CAP,)),
            pltpu.SemaphoreType.DMA((CAP,)),
        ],
        compiler_params=LOCAL,
    )(meta, region, packs, state, table, slots, orep, rrep, oh, kern, *weights)


def shards(
    features,
    positions,
    counts,
    rbf_weight,
    rbf_bias,
    filter_weight,
    filter_bias,
    input_weight,
    output_weight,
    output_bias,
    final_weight,
    final_bias,
):
    state = features.reshape(2 * ATOMS, F)
    table = jnp.asarray(region_table())
    filters = (rbf_weight, rbf_bias, filter_weight, filter_bias)
    atomwise = (output_weight, output_bias, final_weight, final_bias)
    region, packs = start_halo(
        counts.reshape(2), state, positions.reshape(2, 3, ATOMS), input_weight
    )
    state, values, slots, orep, rrep, meta, oh, kern = run_first(
        region, packs, state, table, *filters, *atomwise, input_weight
    )
    region = later_halo(values)
    state = run_second(
        meta, region, packs, state, table, slots, orep, rrep, oh, kern, *filters, *atomwise
    )
    return state.reshape(features.shape)


def solution(mesh):
    cells = P("gx", "gy", "gz", None, None)
    placed = (cells, cells, P("gx", "gy", "gz")) + (P(),) * 9
    return jax.shard_map(
        shards, mesh=mesh, in_specs=placed, out_specs=cells, check_vma=False
    )
```

```python
import math

import jax
import jax.numpy as jnp
import numpy as np
from jax import lax
from jax.experimental import pallas as pl
from jax.experimental.pallas import tpu as pltpu
from jax.sharding import PartitionSpec as P

F = 128
RBF = 64
ATOMS = 64
BLOCKS = 2

cell_edge = 8.0
cutoff = 5.0
gamma = 10.0
scale_sum = 0.125

ROWS = 36 * ATOMS
PACKS = ROWS // F
SLOTS = 512
TILE = 512
CAP = 12
FIXED = 7
HI = lax.Precision.HIGHEST
BF = jnp.bfloat16
VMEM = pl.BlockSpec(memory_space=pltpu.VMEM)
ANY = pl.BlockSpec(memory_space=pl.ANY)
SMEM = pl.BlockSpec(memory_space=pltpu.SMEM)


def softplus(v):
    return jnp.maximum(v, 0.0) + jnp.log(1.0 + jnp.exp(-jnp.abs(v))) - math.log(2.0)


def region_table():
    table = np.zeros((8, ROWS), np.float32)
    for dx in range(3):
        for dy in range(3):
            for k, z in enumerate((0, 1, 2, -1)):
                q = (dx * 3 + dy) * 4 + k
                at = slice(q * ATOMS, (q + 1) * ATOMS)
                table[0, at] = cell_edge * (dx - 1)
                table[1, at] = cell_edge * (dy - 1)
                table[2, at] = cell_edge * z
                table[3, at] = np.arange(ATOMS) + 1 if q == 16 else 100
                table[4, at] = np.arange(ATOMS) + 1 if q == 17 else 100
    return table


def iota(shape, dim):
    return lax.broadcasted_iota(jnp.int32, shape, dim)


def dot(a, b):
    return jnp.dot(a, b, preferred_element_type=jnp.float32)


def pieces3(x):
    a = x.astype(jnp.bfloat16)
    r = x - a.astype(jnp.float32)
    b = r.astype(jnp.bfloat16)
    c = (r - b.astype(jnp.float32)).astype(jnp.bfloat16)
    return a, b, c


def slow_cells(
    b, coords, table_ref, vhl, rw_ref, rb_ref, fw_ref, fb_ref,
    scan_ref, slot_of, oh1, near, w3, orep, rrep, lanes, acc,
):
    acc[...] = jnp.zeros_like(acc)

    @pl.loop(0, 2)
    def _(c):
        base = c * ATOMS
        pick = iota((ATOMS, F), 1) == iota((ATOMS, F), 0) + base
        own = coords[:, 8 * F:9 * F]

        def column(r):
            return jnp.sum(jnp.where(pick, own[r:r + 1, :], 0.0), axis=1, keepdims=True)

        ox, oy, oz, olive = column(0), column(1), column(2), column(3)
        zshift = cell_edge * c.astype(jnp.float32)

        def placed(at):
            px = coords[0:1, at] + table_ref[0:1, at]
            py = coords[1:2, at] + table_ref[1:2, at]
            pz = coords[2:3, at] + (table_ref[2:3, at] - zshift)
            return px, py, pz

        anys = []
        for k in range(PACKS):
            at = slice(k * F, (k + 1) * F)
            px, py, pz = placed(at)
            dx, dy, dz = px - ox, py - oy, pz - oz
            near_enough = jnp.where(dx * dx + dy * dy + dz * dz < cutoff * cutoff, olive, 0.0)
            hit = jnp.max(near_enough, axis=0, keepdims=True) * coords[3:4, at]
            anys.append(jnp.broadcast_to(hit, (8, F)))
        stacked = jnp.concatenate(anys, axis=0)
        scanned = dot(stacked.astype(jnp.bfloat16), scan_ref[...])
        carry = jnp.zeros((8, F), jnp.float32)
        for k in range(PACKS):
            part = scanned[k * 8:(k + 1) * 8]
            slot_of[:, k * F:(k + 1) * F] = jnp.where(
                anys[k] > 0.5, carry + part[:, 0:F] - 1.0, -1.0
            )
            carry = carry + part[:, F:2 * F]
        found = jnp.max(carry).astype(jnp.int32)

        @pl.loop(0, (found + SLOTS - 1) // SLOTS)
        def _(h):
            first = h * SLOTS
            want = (iota((SLOTS, F), 0) + first).astype(jnp.float32)
            for k in range(PACKS):
                at = slice(k * F, (k + 1) * F)
                oh1[:, at] = jnp.where(slot_of[0:1, at] == want, 1.0, 0.0).astype(jnp.bfloat16)
            near[...] = dot(oh1[...], vhl[...]).astype(jnp.bfloat16)
            px, py, pz = placed(slice(0, ROWS))
            ids = table_ref[pl.ds(3 + c, 1), :].astype(jnp.bfloat16)
            rows = [*pieces3(px), *pieces3(py), *pieces3(pz), ids]
            rows = jnp.concatenate(
                [r.astype(jnp.float32) for r in rows] + [jnp.zeros((6, ROWS), jnp.float32)], axis=0
            ).astype(jnp.bfloat16)
            packed = lax.dot_general(
                rows, oh1[...], (((1,), (1,)), ((), ())), preferred_element_type=jnp.float32
            )
            cx = packed[0:1] + packed[1:2] + packed[2:3]
            cy = packed[3:4] + packed[4:5] + packed[5:6]
            cz = packed[6:7] + packed[7:8] + packed[8:9]
            cid = packed[9:10]
            dx, dy, dz = cx - ox, cy - oy, cz - oz
            dist = jnp.sqrt(dx * dx + dy * dy + dz * dz)
            me = (iota((ATOMS, SLOTS), 0) + 1).astype(jnp.float32)
            keep = (dist < cutoff) & (cid > 0.5) & (cid != me) & (olive > 0.5)
            ones = jnp.where(keep, 1.0, 0.0)
            envelope = jnp.where(
                keep, 0.5 * (jnp.cos(math.pi * dist / cutoff) + 1.0), 0.0
            )
            dist = jnp.where(keep, dist, 0.0)
            parts = jnp.concatenate(
                [ones[:, k * F:(k + 1) * F] for k in range(SLOTS // F)], axis=0
            ).astype(jnp.bfloat16)
            scanned = dot(parts, scan_ref[...])
            run = jnp.zeros((ATOMS, F), jnp.float32)
            ranks = []
            for k in range(SLOTS // F):
                part = scanned[k * ATOMS:(k + 1) * ATOMS]
                ranks.append(run + part[:, 0:F])
                run = run + part[:, F:2 * F]
            strict = jnp.where(
                iota((ATOMS, ATOMS), 0) > iota((ATOMS, ATOMS), 1), 1.0, 0.0
            )
            offset = jnp.dot(strict, run, precision=HI, preferred_element_type=jnp.float32)
            orep[...] = offset
            rrep[...] = run
            pairs = jnp.max(offset + run).astype(jnp.int32)
            offset_all = jnp.concatenate([offset] * (SLOTS // F), axis=1)
            index = jnp.where(keep, offset_all + jnp.concatenate(ranks, axis=1), 0.0).astype(
                jnp.int32
            )
            w3[0:64, 0:SLOTS] = (index & ~16383).astype(jnp.float32).astype(jnp.bfloat16)
            w3[64:128, 0:SLOTS] = (index & (127 * 128)).astype(jnp.float32).astype(jnp.bfloat16)
            w3[128:192, 0:SLOTS] = (index & 127).astype(jnp.float32).astype(jnp.bfloat16)
            for n, parts3 in enumerate((pieces3(dist), pieces3(envelope))):
                for r, piece in enumerate(parts3):
                    w3[r * 64:(r + 1) * 64, (n + 1) * SLOTS:(n + 2) * SLOTS] = piece
            w3[192:256, :] = jnp.zeros((64, 3 * SLOTS), jnp.bfloat16)
            spread = ((iota((ATOMS, 2 * F), 1) & 63) == iota((ATOMS, 2 * F), 0)) & (
                iota((ATOMS, 2 * F), 1) < 192
            )
            two = jnp.concatenate([offset, offset], axis=1)
            low = jnp.sum(jnp.where(spread, two, 0.0), axis=0, keepdims=True)
            two = jnp.concatenate([run, run], axis=1)
            count = jnp.sum(jnp.where(spread, two, 0.0), axis=0, keepdims=True)
            lanes[0:1, :] = low
            lanes[1:2, :] = low + count

            @pl.loop(0, (pairs + TILE - 1) // TILE)
            def _(t):
                start = (t * TILE).astype(jnp.float32)
                p = iota((TILE, 2 * F), 0).astype(jnp.float32) + start
                member = jnp.where((lanes[0:1, :] <= p) & (p < lanes[1:2, :]), 1.0, 0.0)
                member = member.astype(jnp.bfloat16)
                p1 = iota((TILE, SLOTS), 0).astype(jnp.float32) + (start + 1.0)
                hot = dot(member, w3[:, 0:SLOTS]) == p1
                d = jnp.sum(
                    jnp.where(hot, dot(member, w3[:, SLOTS:2 * SLOTS]), 0.0), axis=1, keepdims=True
                )
                e = jnp.sum(
                    jnp.where(hot, dot(member, w3[:, 2 * SLOTS:3 * SLOTS]), 0.0),
                    axis=1,
                    keepdims=True,
                )
                onehot = jnp.where(hot, 1.0, 0.0).astype(jnp.bfloat16)
                got = dot(onehot, near[...])
                got = got[:, 0:F] + got[:, F:2 * F]
                centres = iota((TILE, RBF), 1).astype(jnp.float32) * (cutoff / (RBF - 1))
                apart = d - centres
                radial = jnp.exp(-gamma * apart * apart).astype(jnp.bfloat16)
                hidden = softplus(dot(radial, rw_ref[b]) + rb_ref[b:b + 1]).astype(jnp.bfloat16)
                kern = ((dot(hidden, fw_ref[b]) + fb_ref[b:b + 1]) * e).astype(jnp.bfloat16)
                prod = kern.astype(jnp.float32) * got
                top = prod.astype(jnp.bfloat16)
                rest = (prod - top.astype(jnp.float32)).astype(jnp.bfloat16)
                pl_ = iota((ATOMS, TILE), 1).astype(jnp.float32) + start
                lo = jnp.concatenate([orep[...]] * (TILE // F), axis=1)
                hi = lo + jnp.concatenate([rrep[...]] * (TILE // F), axis=1)
                back = jnp.where((lo <= pl_) & (pl_ < hi), 1.0, 0.0).astype(jnp.bfloat16)
                summed = dot(back, jnp.concatenate([top, rest], axis=1))
                at = pl.ds(pl.multiple_of(base, ATOMS), ATOMS)
                acc[at, :] += summed[:, 0:F] + summed[:, F:2 * F]


def dense(x, w):
    return jnp.dot(x, w, precision=HI, preferred_element_type=jnp.float32)


def region_rows(dx, dy, k, cells):
    return pl.ds((((dx + 1) * 3 + dy + 1) * 4 + k) * ATOMS, cells * ATOMS)


def neighbours():
    return [
        (ox, oy, oz)
        for ox in (-1, 0, 1)
        for oy in (-1, 0, 1)
        for oz in (-1, 0, 1)
        if (ox, oy, oz) != (0, 0, 0)
    ]


def device_at(offset):
    return tuple(
        lax.rem(lax.axis_index(a) + (o + lax.axis_size(a)), lax.axis_size(a))
        for a, o in zip(("gx", "gy", "gz"), offset)
    )


def greet(offsets):
    barrier = pltpu.get_barrier_semaphore()
    for o in offsets:
        pl.semaphore_signal(
            barrier, inc=1, device_id=device_at(o), device_id_type=pl.DeviceIdType.MESH
        )
    pl.semaphore_wait(barrier, len(offsets))


FACES = [(0, 1, 0), (0, -1, 0), (0, 0, 1), (0, 0, -1), (1, 0, 0), (-1, 0, 0)]


def spread_steps(vals, region, ssem, rsem):
    copies = {}

    def send(name, src, dst, to):
        n = len(copies)
        copies[name] = pltpu.make_async_remote_copy(
            src_ref=src,
            dst_ref=region.at[dst],
            send_sem=ssem.at[n],
            recv_sem=rsem.at[n],
            device_id=device_at(to),
            device_id_type=pl.DeviceIdType.MESH,
        )
        copies[name].start()

    def cells(dy, k, n):
        if dy == 0 and k < 2:
            return vals.at[pl.ds(k * ATOMS, n * ATOMS)]
        return region.at[region_rows(0, dy, k, n)]

    def send_z(dy):
        send(("z", dy, 3), cells(dy, 1, 1), region_rows(0, dy, 3, 1), (0, 0, 1))
        send(("z", dy, 2), cells(dy, 0, 1), region_rows(0, dy, 2, 1), (0, 0, -1))

    def send_x(dy, k):
        send(("x", dy, k, 1), cells(dy, k, 2), region_rows(-1, dy, k, 2), (1, 0, 0))
        send(("x", dy, k, -1), cells(dy, k, 2), region_rows(1, dy, k, 2), (-1, 0, 0))

    send(("y", -1), cells(0, 0, 2), region_rows(0, -1, 0, 2), (0, 1, 0))
    send(("y", 1), cells(0, 0, 2), region_rows(0, 1, 0, 2), (0, -1, 0))
    send_z(0)
    send_x(0, 0)
    region[region_rows(0, 0, 0, 2), :] = vals[...]
    yield
    for k in (2, 3):
        copies["z", 0, k].wait_recv()
    send_x(0, 2)
    for dy in (-1, 1):
        copies["y", dy].wait_recv()
        send_z(dy)
        send_x(dy, 0)
    yield
    for dy in (-1, 1):
        for k in (2, 3):
            copies["z", dy, k].wait_recv()
        send_x(dy, 2)
    yield
    for name, copy in copies.items():
        if name[0] == "x":
            copy.wait_recv()
    for copy in copies.values():
        copy.wait_send()
    yield


def split_values(region, vhl):
    @pl.loop(0, ROWS // 256)
    def _(k):
        at = pl.ds(pl.multiple_of(k * 256, 256), 256)
        v = region[at, :]
        top = v.astype(jnp.bfloat16)
        vhl[at, 0:F] = top
        vhl[at, F:2 * F] = (v - top.astype(jnp.float32)).astype(jnp.bfloat16)


def place_packs(packs, coords):
    lower = iota((8, F), 1) < ATOMS
    for q in range(9):
        coords[:, 2 * q * F:(2 * q + 1) * F] = packs[3 * q + 1]
        coords[:, (2 * q + 1) * F:(2 * q + 2) * F] = jnp.where(
            lower, packs[3 * q + 2], packs[3 * q]
        )


def fill_scan(scan):
    upper = iota((F, F), 0) <= iota((F, F), 1)
    scan[:, 0:F] = jnp.where(upper, 1.0, 0.0).astype(jnp.bfloat16)
    scan[:, F:2 * F] = jnp.ones((F, F), jnp.bfloat16)


def finish(b, coords, state_ref, acc, ow, ob, nw, nb):
    mixed = softplus(dense(acc[...] * scale_sum, ow[b]) + ob[b:b + 1])
    update = dense(mixed, nw[b]) + nb[b:b + 1]
    diag = iota((F, F), 0) == iota((F, F), 1)
    live = jnp.sum(jnp.where(diag, coords[3:4, 8 * F:9 * F], 0.0), axis=1, keepdims=True)
    return (state_ref[...] + update) * live


def add_pairs(onehot, kern, near, low, size, start):
    got = dot(onehot, near)
    got = got[:, 0:F] + got[:, F:2 * F]
    prod = kern.astype(jnp.float32) * got
    top = prod.astype(jnp.bfloat16)
    rest = (prod - top.astype(jnp.float32)).astype(jnp.bfloat16)
    p = iota((ATOMS, TILE), 1).astype(jnp.float32) + start
    lo = jnp.concatenate([low] * (TILE // F), axis=1)
    hi = lo + jnp.concatenate([size] * (TILE // F), axis=1)
    back = jnp.where((lo <= p) & (p < hi), 1.0, 0.0).astype(jnp.bfloat16)
    summed = dot(back, jnp.concatenate([top, rest], axis=1))
    return summed[:, 0:F] + summed[:, F:2 * F]


def hot_rows(slots, c):
    want = iota((SLOTS, F), 0).astype(jnp.float32)
    return jnp.concatenate(
        [
            jnp.where(slots[pl.ds(8 * c, 1), k * F:(k + 1) * F] == want, 1.0, 0.0).astype(BF)
            for k in range(PACKS)
        ],
        axis=1,
    )


def place_table(coords, table, turned):
    for g in range(PACKS):
        at = slice(g * F, (g + 1) * F)
        parts = [p.astype(jnp.float32) for p in pieces3(coords[:, at])]
        rows = jnp.concatenate([*parts, table[:, at], jnp.zeros((96, F), jnp.float32)], axis=0)
        turned[at, :] = rows.T.astype(BF)


def half_wave(dist):
    x = dist * (math.pi / (2.0 * cutoff))
    y = x * x
    total = jnp.full_like(y, 1.0 / math.factorial(12))
    for n in (10, 8, 6, 4, 2, 0):
        total = total * y + (-1.0) ** (n // 2) / math.factorial(n)
    return total * total


def prepare(c, coords, table, turned, scan, slots, rank2, dist2, lanes2, orep2, rrep2, totals):
    base = c * ATOMS
    pick = iota((ATOMS, F), 1) == iota((ATOMS, F), 0) + base
    own = coords[:, 8 * F:9 * F]

    def column(r):
        return jnp.sum(jnp.where(pick, own[r:r + 1, :], 0.0), axis=1, keepdims=True)

    ox, oy, oz, olive = column(0), column(1), column(2), column(3)
    zshift = cell_edge * c
    anys = []
    for k in range(PACKS):
        at = slice(k * F, (k + 1) * F)
        dx = coords[0:1, at] + table[0:1, at] - ox
        dy = coords[1:2, at] + table[1:2, at] - oy
        dz = coords[2:3, at] + (table[2:3, at] - zshift) - oz
        near_enough = jnp.where(dx * dx + dy * dy + dz * dz < cutoff * cutoff, olive, 0.0)
        hit = jnp.max(near_enough, axis=0, keepdims=True) * coords[3:4, at]
        anys.append(jnp.broadcast_to(hit, (8, F)))
    scanned = dot(jnp.concatenate(anys, axis=0).astype(BF), scan[...])
    carry = jnp.zeros((8, F), jnp.float32)
    for k in range(PACKS):
        part = scanned[k * 8:(k + 1) * 8]
        slots[8 * c:8 * c + 8, k * F:(k + 1) * F] = jnp.where(
            anys[k] > 0.5, carry + part[:, 0:F] - 1.0, -1.0
        )
        carry = carry + part[:, F:2 * F]
    totals[2 * c:2 * c + 1, :] = carry[0:1]
    found = dot(hot_rows(slots, c), turned[...])
    packed = jnp.concatenate(
        [found[k * F:(k + 1) * F].T[0:32] for k in range(SLOTS // F)], axis=1
    )
    cx = packed[0:1] + packed[8:9] + packed[16:17] + packed[24:25]
    cy = packed[1:2] + packed[9:10] + packed[17:18] + packed[25:26]
    cz = packed[2:3] + packed[10:11] + packed[18:19] + (packed[26:27] - zshift)
    cid = packed[27 + c:28 + c]
    dx, dy, dz = cx - ox, cy - oy, cz - oz
    dist = jnp.sqrt(dx * dx + dy * dy + dz * dz)
    me = (iota((ATOMS, SLOTS), 0) + 1).astype(jnp.float32)
    keep = (dist < cutoff) & (cid > 0.5) & (cid != me) & (olive > 0.5)
    ones = jnp.where(keep, 1.0, 0.0)
    dist = jnp.where(keep, dist, 0.0)
    both = jnp.concatenate([dist, jnp.where(keep, half_wave(dist), 0.0)], axis=0)
    for k in range(SLOTS // F):
        at = slice(k * F, (k + 1) * F)
        flipped = both[:, at].T
        top = flipped.astype(BF)
        dist2[c, at, 0:F] = top
        dist2[c, at, F:2 * F] = (flipped - top.astype(jnp.float32)).astype(BF)
    parts = jnp.concatenate([ones[:, k * F:(k + 1) * F] for k in range(SLOTS // F)], axis=0)
    scanned = dot(parts.astype(BF), scan[...])
    run = jnp.zeros((ATOMS, F), jnp.float32)
    ranks = []
    for k in range(SLOTS // F):
        part = scanned[k * ATOMS:(k + 1) * ATOMS]
        ranks.append(run + part[:, 0:F])
        run = run + part[:, F:2 * F]
    strict = jnp.where(iota((ATOMS, ATOMS), 0) > iota((ATOMS, ATOMS), 1), 1.0, 0.0)
    offset = jnp.dot(strict, run, precision=HI, preferred_element_type=jnp.float32)
    orep2[c] = offset
    rrep2[c] = run
    totals[2 * c + 1:2 * c + 2, :] = (offset + run)[ATOMS - 1:ATOMS]
    offset_all = jnp.concatenate([offset] * (SLOTS // F), axis=1)
    index = jnp.where(keep, offset_all + jnp.concatenate(ranks, axis=1), 0.0).astype(jnp.int32)
    rank2[c, 0:64, :] = (index & ~255).astype(jnp.float32).astype(BF)
    rank2[c, 64:128, :] = (index & 255).astype(jnp.float32).astype(BF)
    spread = (iota((ATOMS, F), 1) & 63) == iota((ATOMS, F), 0)
    low = jnp.sum(jnp.where(spread, offset, 0.0), axis=0, keepdims=True)
    count = jnp.sum(jnp.where(spread, run, 0.0), axis=0, keepdims=True)
    lanes2[c, 0:1, :] = low
    lanes2[c, 1:2, :] = low + count


def make_pairs(c, t, rank2, dist2, lanes2):
    start = (t * TILE).astype(jnp.float32)
    p = iota((TILE, F), 0).astype(jnp.float32) + start
    member = (lanes2[c, 0:1, :] <= p) & (p < lanes2[c, 1:2, :])
    member_of = jnp.where(member, 1.0, 0.0).astype(BF)
    p1 = iota((TILE, SLOTS), 0).astype(jnp.float32) + (start + 1.0)
    hot = dot(member_of, rank2[c]) == p1
    onehot = jnp.where(hot, 1.0, 0.0).astype(BF)
    seen = dot(onehot, dist2[c])
    seen = jnp.where(member, seen[:, 0:F] + seen[:, F:2 * F], 0.0)
    half = iota((TILE, F), 1) < RBF
    d = jnp.sum(jnp.where(half, seen, 0.0), axis=1, keepdims=True)
    e = jnp.sum(jnp.where(half, 0.0, seen), axis=1, keepdims=True)
    centres = iota((TILE, F), 1).astype(jnp.float32) * (cutoff / (RBF - 1))
    apart = d - centres
    return onehot, jnp.where(half, jnp.exp(-gamma * apart * apart), e), e


def make_filter(b, radial, e, rw_wide, rb, fw, fb):
    hidden = dot(radial.astype(BF), rw_wide[...])
    log2e = math.log2(math.e)
    grown = jnp.exp2(hidden * log2e + (rb[b:b + 1] * log2e - 1.0))
    hidden = jnp.log(grown + 0.5).astype(BF)
    return ((dot(hidden, fw[b]) + fb[b:b + 1]) * e).astype(BF)


def fill_wide(b, rw, rw_wide):
    rw_wide[0:RBF, :] = rw[b]
    rw_wide[RBF:F, :] = jnp.zeros((RBF, F), BF)


def rows_of(c, t):
    return pl.ds(pl.multiple_of((c * CAP + t) * TILE, TILE), TILE)


def first_comm(
    counts_ref, state_ref, pos_ref, iw_ref, table, rw, rb, fw, fb,
    region, coords, slots, orep2, rrep2, lanes2, rank2, dist2, totals,
    oh_hbm, kern0_hbm, rad_hbm,
    vals, pack, packs, turned, scan, rw_wide, oh_all, kern0_all, rad_all,
    ssem, rsem, psend, precv, osem, k0sem, k1sem,
):
    live = [jnp.where(iota((1, ATOMS), 1) < counts_ref[c], 1.0, 0.0) for c in range(2)]
    rows = [
        jnp.concatenate([pos_ref[0, c:c + 1], pos_ref[1, c:c + 1], pos_ref[2, c:c + 1], live[c], jnp.zeros((4, ATOMS), jnp.float32)], axis=0)
        for c in range(2)
    ]
    pack[...] = jnp.concatenate(rows, axis=1)
    greet(neighbours())
    copies = []
    for n, (ox, oy, oz) in enumerate(neighbours()):
        slot = (1 - ox) * 9 + (1 - oy) * 3 + (1 - oz)
        copies.append(
            pltpu.make_async_remote_copy(
                src_ref=pack,
                dst_ref=packs.at[slot],
                send_sem=psend.at[n],
                recv_sem=precv.at[n],
                device_id=device_at((ox, oy, oz)),
                device_id_type=pl.DeviceIdType.MESH,
            )
        )
        copies[-1].start()
    packs[13] = pack[...]
    vals[...] = dense(state_ref[...], iw_ref[0])
    fill_scan(scan)
    fill_wide(0, rw, rw_wide)
    totals[...] = jnp.zeros_like(totals)
    lanes2[...] = jnp.zeros_like(lanes2)
    steps = spread_steps(vals, region, ssem, rsem)
    next(steps)
    next(steps)
    for copy in copies:
        copy.wait_recv()
    place_packs(packs, coords)
    place_table(coords, table, turned)
    for c in range(2):
        prepare(
            c, coords, table, turned, scan, slots, rank2, dist2, lanes2, orep2, rrep2, totals
        )

    def out(c, t):
        n = c * FIXED + t
        here = pl.ds(pl.multiple_of(n * TILE, TILE), TILE)
        return (
            pltpu.make_async_copy(oh_all.at[here], oh_hbm.at[rows_of(c, t)], osem.at[n]),
            pltpu.make_async_copy(kern0_all.at[here], kern0_hbm.at[rows_of(c, t)], k0sem.at[n]),
            pltpu.make_async_copy(rad_all.at[here], rad_hbm.at[here], k1sem.at[n]),
        )

    def tiles(first, last):
        @pl.loop(first, last)
        def _(t):
            made = [make_pairs(c, t, rank2, dist2, lanes2) for c in range(2)]
            kerns = [make_filter(0, radial, e, rw_wide, rb, fw, fb) for _, radial, e in made]
            for c in range(2):
                here = pl.ds(pl.multiple_of((c * FIXED + t) * TILE, TILE), TILE)
                oh_all[here, :] = made[c][0]
                rad_all[here, :] = made[c][1]
                kern0_all[here, :] = kerns[c]
                for copy in out(c, t):
                    copy.start()

    tiles(0, 1)
    next(steps)
    tiles(1, FIXED)
    next(steps)
    for copy in copies:
        copy.wait_send()

    @pl.loop(0, 2 * FIXED)
    def _(n):
        c = n // FIXED
        for copy in out(c, n - c * FIXED):
            copy.wait()


def later_comm(
    vals_ref, rad_hbm, rw, rb, fw, fb, region, kern1, rad_all, rw_wide, ssem, rsem, isem
):
    def fetch(n):
        here = pl.ds(pl.multiple_of(n * TILE, TILE), TILE)
        return pltpu.make_async_copy(rad_hbm.at[here], rad_all.at[here], isem.at[n])

    @pl.loop(0, 2 * FIXED)
    def _(n):
        fetch(n).start()

    fill_wide(1, rw, rw_wide)
    greet(FACES)
    steps = spread_steps(vals_ref, region, ssem, rsem)
    next(steps)

    def tiles(first, last):
        @pl.loop(first, last)
        def _(n):
            fetch(n).wait()
            here = pl.ds(pl.multiple_of(n * TILE, TILE), TILE)
            radial = rad_all[here, :]
            kern1[here, :] = make_filter(1, radial, radial[:, RBF:RBF + 1], rw_wide, rb, fw, fb)

    tiles(0, 8)
    next(steps)
    tiles(8, 2 * FIXED)
    next(steps)
    next(steps)


def later_halo(vals, radial, *filters):
    return pl.pallas_call(
        later_comm,
        out_shape=(REGION, FIXED_KERN),
        in_specs=[VMEM, ANY] + [VMEM] * 4,
        out_specs=(VMEM, VMEM),
        scratch_shapes=[
            pltpu.VMEM((2 * FIXED * TILE, F), jnp.float32),
            pltpu.VMEM((F, F), BF),
            pltpu.SemaphoreType.DMA((20,)),
            pltpu.SemaphoreType.DMA((20,)),
            pltpu.SemaphoreType.DMA((2 * FIXED,)),
        ],
        compiler_params=pltpu.CompilerParams(
            collective_id=1, has_side_effects=True, vmem_limit_bytes=WHOLE
        ),
    )(vals, radial, *filters)


def sizes(totals):
    found = jnp.maximum(jnp.max(totals[0:1, :]), jnp.max(totals[2:3, :])).astype(jnp.int32)
    many = [
        (jnp.max(totals[2 * c + 1:2 * c + 2, :]).astype(jnp.int32) + TILE - 1) // TILE
        for c in range(2)
    ]
    fits = (found <= SLOTS) & (many[0] <= CAP) & (many[1] <= CAP)
    return fits, [jnp.where(fits, m, 0) for m in many]


def use_tiles(many, near2, oh_all, kern_all, orep2, rrep2, acc, before):
    @pl.loop(0, 2)
    def _(c):
        count = jnp.where(c == 0, many[0], many[1])

        @pl.loop(0, (count + 1) // 2)
        def _(pair):
            first = 2 * pair
            second = jnp.minimum(first + 1, count - 1)
            before(c, first)

            @pl.when(second > first)
            def _():
                before(c, second)

            rows = pl.ds(pl.multiple_of(c * ATOMS, ATOMS), ATOMS)
            total = 0.0
            for t, n in ((first, first), (second, first + 1)):
                at = rows_of(c, t)
                total = total + add_pairs(
                    oh_all[at, :], kern_all[at, :], near2[c], orep2[c], rrep2[c],
                    (n * TILE).astype(jnp.float32),
                )
            acc[rows, :] += total


def first_block(
    totals, region, coords, state_ref, table_ref, slots, orep2, rrep2, lanes2, rank2, dist2,
    oh_in, kern0_hbm,
    rw, rb, fw, fb, ow, ob, nw, nb, iw,
    out_ref, next_ref, oh_hbm, kern1_hbm,
    vhl, scan, oh1, near2, acc, oh_all, kern0_all, kern1_all,
    rw_wide, rw_wide1, slot_s, w3, orep, rrep, lanes, osem, ksem,
):
    fits, many = sizes(totals)

    def fetch(c, t):
        n, at = c * CAP + t, rows_of(c, t)
        return (
            pltpu.make_async_copy(oh_hbm.at[at], oh_all.at[at], osem.at[n]),
            pltpu.make_async_copy(kern0_hbm.at[at], kern0_all.at[at], ksem.at[n]),
        )

    def put(c, t):
        n, at = c * CAP + t, rows_of(c, t)
        return (
            pltpu.make_async_copy(oh_all.at[at], oh_hbm.at[at], osem.at[n]),
            pltpu.make_async_copy(kern1_all.at[at], kern1_hbm.at[at], ksem.at[n]),
        )

    for c in range(2):
        @pl.loop(0, jnp.minimum(many[c], FIXED))
        def _(t):
            for copy in fetch(c, t):
                copy.start()

    split_values(region, vhl)
    acc[...] = jnp.zeros_like(acc)

    @pl.when(fits)
    def _():
        @pl.loop(0, 2)
        def _(c):
            near2[c] = dot(hot_rows(slots, c), vhl[...]).astype(BF)

        @pl.when((many[0] > FIXED) | (many[1] > FIXED))
        def _():
            fill_wide(0, rw, rw_wide)
            fill_wide(1, rw, rw_wide1)

        def before(c, t):
            @pl.when(t < FIXED)
            def _():
                for copy in fetch(c, t):
                    copy.wait()

            @pl.when(t >= FIXED)
            def _():
                at = rows_of(c, t)
                onehot, radial, e = make_pairs(c, t, rank2, dist2, lanes2)
                oh_all[at, :] = onehot
                kern0_all[at, :] = make_filter(0, radial, e, rw_wide, rb, fw, fb)
                kern1_all[at, :] = make_filter(1, radial, e, rw_wide1, rb, fw, fb)
                for copy in put(c, t):
                    copy.start()

        use_tiles(many, near2, oh_all, kern0_all, orep2, rrep2, acc, before)

    @pl.when(jnp.logical_not(fits))
    def _():
        fill_scan(scan)
        slow_cells(
            0, coords, table_ref, vhl, rw, rb, fw, fb,
            scan, slot_s, oh1, near2.at[0], w3, orep, rrep, lanes, acc,
        )

    state = finish(0, coords, state_ref, acc, ow, ob, nw, nb)
    out_ref[...] = state
    next_ref[...] = dense(state, iw[1])
    for c in range(2):
        @pl.loop(FIXED, jnp.maximum(many[c], FIXED))
        def _(t):
            for copy in put(c, t):
                copy.wait()


def second_block(
    totals, region, coords, state_ref, table_ref, slots, orep2, rrep2, oh_hbm, fixed1_hbm, kern1_hbm,
    rw, rb, fw, fb, ow, ob, nw, nb,
    out_ref,
    vhl, scan, oh1, near2, acc, oh_all, kern_all, slot_s, w3, orep, rrep, lanes,
    osem, ksem,
):
    fits, many = sizes(totals)

    def fetch(c, t, fixed):
        n, at = c * CAP + t, rows_of(c, t)
        source = kern1_hbm.at[at]
        if fixed:
            source = fixed1_hbm.at[pl.ds(pl.multiple_of((c * FIXED + t) * TILE, TILE), TILE)]
        return (
            pltpu.make_async_copy(oh_hbm.at[at], oh_all.at[at], osem.at[n]),
            pltpu.make_async_copy(source, kern_all.at[at], ksem.at[n]),
        )

    for c in range(2):
        @pl.loop(0, jnp.minimum(many[c], FIXED))
        def _(t):
            for copy in fetch(c, t, True):
                copy.start()

        @pl.loop(FIXED, jnp.maximum(many[c], FIXED))
        def _(t):
            for copy in fetch(c, t, False):
                copy.start()

    split_values(region, vhl)
    acc[...] = jnp.zeros_like(acc)

    @pl.when(fits)
    def _():
        @pl.loop(0, 2)
        def _(c):
            near2[c] = dot(hot_rows(slots, c), vhl[...]).astype(BF)

        def before(c, t):
            for copy in fetch(c, t, False):
                copy.wait()

        use_tiles(many, near2, oh_all, kern_all, orep2, rrep2, acc, before)

    @pl.when(jnp.logical_not(fits))
    def _():
        fill_scan(scan)
        slow_cells(
            1, coords, table_ref, vhl, rw, rb, fw, fb,
            scan, slot_s, oh1, near2.at[0], w3, orep, rrep, lanes, acc,
        )

    out_ref[...] = finish(1, coords, state_ref, acc, ow, ob, nw, nb)


STATE = jax.ShapeDtypeStruct((2 * ATOMS, F), jnp.float32)
REGION = jax.ShapeDtypeStruct((ROWS, F), jnp.float32)
BIG = 2 * CAP * TILE
HOT = jax.ShapeDtypeStruct((BIG, SLOTS), BF)
KERN = jax.ShapeDtypeStruct((BIG, F), BF)
RADIAL = jax.ShapeDtypeStruct((2 * FIXED * TILE, F), jnp.float32)
FIXED_KERN = jax.ShapeDtypeStruct((2 * FIXED * TILE, F), BF)
WHOLE = 60 << 20


def start_halo(counts, state, positions, input_weight, table, *filters):
    return pl.pallas_call(
        first_comm,
        out_shape=(
            REGION,
            jax.ShapeDtypeStruct((8, ROWS), jnp.float32),
            jax.ShapeDtypeStruct((16, ROWS), jnp.float32),
            jax.ShapeDtypeStruct((2, ATOMS, F), jnp.float32),
            jax.ShapeDtypeStruct((2, ATOMS, F), jnp.float32),
            jax.ShapeDtypeStruct((2, 8, F), jnp.float32),
            jax.ShapeDtypeStruct((2, F, SLOTS), BF),
            jax.ShapeDtypeStruct((2, SLOTS, 2 * F), BF),
            jax.ShapeDtypeStruct((8, F), jnp.float32),
            HOT,
            KERN,
            RADIAL,
        ),
        in_specs=[SMEM] + [VMEM] * 8,
        out_specs=(VMEM,) * 9 + (ANY,) * 3,
        scratch_shapes=[
            pltpu.VMEM((2 * ATOMS, F), jnp.float32),
            pltpu.VMEM((8, F), jnp.float32),
            pltpu.VMEM((27, 8, F), jnp.float32),
            pltpu.VMEM((ROWS, F), BF),
            pltpu.VMEM((F, 2 * F), BF),
            pltpu.VMEM((F, F), BF),
            pltpu.VMEM((2 * FIXED * TILE, SLOTS), BF),
            pltpu.VMEM((2 * FIXED * TILE, F), BF),
            pltpu.VMEM((2 * FIXED * TILE, F), jnp.float32),
            pltpu.SemaphoreType.DMA((20,)),
            pltpu.SemaphoreType.DMA((20,)),
            pltpu.SemaphoreType.DMA((26,)),
            pltpu.SemaphoreType.DMA((26,)),
            pltpu.SemaphoreType.DMA((2 * FIXED,)),
            pltpu.SemaphoreType.DMA((2 * FIXED,)),
            pltpu.SemaphoreType.DMA((2 * FIXED,)),
        ],
        compiler_params=pltpu.CompilerParams(
            collective_id=0, has_side_effects=True, vmem_limit_bytes=WHOLE
        ),
    )(counts, state, positions, input_weight, table, *filters)


GENERAL = [
    pltpu.VMEM((8, ROWS), jnp.float32),
    pltpu.VMEM((256, 3 * SLOTS), BF),
    pltpu.VMEM((ATOMS, F), jnp.float32),
    pltpu.VMEM((ATOMS, F), jnp.float32),
    pltpu.VMEM((8, 2 * F), jnp.float32),
    pltpu.SemaphoreType.DMA((2 * CAP,)),
    pltpu.SemaphoreType.DMA((2 * CAP,)),
]
SHARED = [
    pltpu.VMEM((ROWS, 2 * F), BF),
    pltpu.VMEM((F, 2 * F), BF),
    pltpu.VMEM((SLOTS, ROWS), BF),
    pltpu.VMEM((2, SLOTS, 2 * F), BF),
    pltpu.VMEM((2 * ATOMS, F), jnp.float32),
    pltpu.VMEM((BIG, SLOTS), BF),
    pltpu.VMEM((BIG, F), BF),
]


def run_first(*args):
    return pl.pallas_call(
        first_block,
        out_shape=(STATE, STATE, HOT, KERN),
        in_specs=[VMEM] * 11 + [ANY] * 2 + [VMEM] * 9,
        out_specs=(VMEM, VMEM, ANY, ANY),
        input_output_aliases={11: 2},
        scratch_shapes=SHARED
        + [
            pltpu.VMEM((BIG, F), BF),
            pltpu.VMEM((F, F), BF),
            pltpu.VMEM((F, F), BF),
        ]
        + GENERAL,
        compiler_params=pltpu.CompilerParams(vmem_limit_bytes=WHOLE),
    )(*args)


def run_second(*args):
    return pl.pallas_call(
        second_block,
        out_shape=STATE,
        in_specs=[VMEM] * 8 + [ANY] * 3 + [VMEM] * 8,
        out_specs=VMEM,
        scratch_shapes=SHARED + GENERAL,
        compiler_params=pltpu.CompilerParams(vmem_limit_bytes=WHOLE),
    )(*args)


def shards(
    features,
    positions,
    counts,
    rbf_weight,
    rbf_bias,
    filter_weight,
    filter_bias,
    input_weight,
    output_weight,
    output_bias,
    final_weight,
    final_bias,
):
    state = features.reshape(2 * ATOMS, F)
    table = jnp.asarray(region_table())
    filters = (rbf_weight, rbf_bias, filter_weight, filter_bias)
    atomwise = (output_weight, output_bias, final_weight, final_bias)
    region, coords, slots, orep, rrep, lanes, rank, dist, totals, oh, kern0, radial = start_halo(
        counts.reshape(2), state, jnp.transpose(positions.reshape(2, 3, ATOMS), (1, 0, 2)), input_weight, table, *filters
    )
    state, values, oh, kern1 = run_first(
        totals, region, coords, state, table, slots, orep, rrep, lanes, rank, dist,
        oh, kern0, *filters, *atomwise, input_weight,
    )
    region, fixed1 = later_halo(values, radial, *filters)
    state = run_second(
        totals, region, coords, state, table, slots, orep, rrep, oh, fixed1, kern1, *filters, *atomwise
    )
    return state.reshape(features.shape)


def solution(mesh):
    cells = P("gx", "gy", "gz", None, None)
    placed = (cells, cells, P("gx", "gy", "gz")) + (P(),) * 9
    return jax.shard_map(
        shards, mesh=mesh, in_specs=placed, out_specs=cells, check_vma=False
    )
```
